128 devices in a mesh: seq: 32 (over y, x, core), mp: 4 (over z).
Axes of the slice: x: 4, y: 4, z: 4, core: 2. Of those that a mesh axis runs over, the one named last changes fastest.
Arguments:
- y_first: bfloat16 [8192, 4096], P('seq', 'mp'), may hold values from -6 to 6
- x_second: bfloat16 [8192, 4096], P('seq', 'mp'), may hold values from -6 to 6
- grad_first: bfloat16 [8192, 4096], P('seq', 'mp'), may hold values from -6 to 6
- grad_second: bfloat16 [8192, 4096], P('seq', 'mp'), may hold values from -6 to 6
- doc_ids: int32 [8192], P('seq'), may hold values from 0 to 7, never falling along the last dimension, each value on 1 to 4096 neighbouring positions
- norm_gain: float32 [4096], replicated, may hold values from 0.25 to 1.75
- w_query: bfloat16 [4096, 2048], P(None, 'mp'), may hold values from -2 to 2
- w_key: bfloat16 [4096, 512], P(None, 'mp'), may hold values from -2 to 2
- w_value: bfloat16 [4096, 512], P(None, 'mp'), may hold values from -0.09375 to 0.09375
- w_out: bfloat16 [2048, 4096], P('mp'), may hold values from -0.25 to 0.25
Outputs:
- x_first: float32 [8192, 4096], P('seq', 'mp')
- x_grad: float32 [8192, 4096], P('seq', 'mp')
The draws below stay inside these ranges and needn't reach their ends.
Inputs may be any that keep to these rules, and one draw needn't show every extreme that they name: `doc_ids`: document numbers never fall along the sequence; every document has 1 to 4096 tokens, and one has exactly 4096.
All inputs are finite; a program needn't handle non-finite values.
Results may differ from the reference program's by a relative error of at most 0.0092.
Values may be sent and summed in bfloat16 or wider, within the bound.
A program may use at most 128 MiB of HBM per device.

```python
import math
import jax
import jax.numpy as jnp
import numpy as np
from jax import lax

D = 4096
HEAD_DIM = 128
HEADS = 16
KV_HEADS = 4
DOCS = 8
TOKENS = 8192


def paired_weights(key):
    base_keys = jax.random.normal(jax.random.fold_in(key, 11), (D, KV_HEADS * HEAD_DIM), jnp.float32) * D ** (-0.5)
    noise = jax.random.normal(jax.random.fold_in(key, 12), (D, HEADS * HEAD_DIM), jnp.float32) * (2.0 * D ** (-0.5))
    query_part = noise
    return (jnp.clip(base_keys, -2.0, 2.0), jnp.clip(query_part, -2.0, 2.0))


def draw_w_query(key, part):
    return paired_weights(key)[1].astype(jnp.bfloat16)


def draw_w_key(key, part):
    return paired_weights(key)[0].astype(jnp.bfloat16)


def block_levels(key, dims, split, smallest, high):
    gain = 1.0
    for position, parts in split:
        draws = jax.random.uniform(jax.random.fold_in(jax.random.fold_in(key, 6), position), (parts,), jnp.float32, smallest / len(split), high / len(split))
        gain = gain * jnp.repeat(jnp.exp(draws), dims[position] // parts).reshape((-1,) + (1,) * (len(dims) - 1 - position))
    return gain


def length_profile(count, total, bound, slope):
    weights = [(1 << 20) // math.isqrt(grade ** slope) + 1 for grade in range(2, count + 1)]
    spare, holding = total - bound - (count - 1), [1] * (count - 1)
    while spare > 0:
        free = [i for i in range(count - 1) if holding[i] < bound]
        pool, remaining = sum([weights[i] for i in free]), spare
        for i in free:
            addition = min(bound - holding[i], max(1, remaining * weights[i] // pool), spare)
            holding[i] = holding[i] + addition
            spare = spare - addition
    return np.array([bound] + holding)


def ragged_sizes(key, amount, total, most, slope):
    if amount == 2:
        one = jax.random.randint(key, (), max(1, total - most), min(most, total - 1) + 1)
        return jnp.stack([one, total - one])
    lengths = jnp.asarray(length_profile(amount, total, most, slope), jnp.int32)
    twos = (amount - 1) // 2
    donor, sink = lengths[1:1 + 2 * twos:2], lengths[2:2 + 2 * twos:2]
    room = jnp.minimum(donor - 1, most - sink)
    shifted = jax.random.randint(jax.random.fold_in(key, 1), (twos,), 0, 1 << 20) % (room + 1)
    lengths = lengths.at[1:1 + 2 * twos:2].set(donor - shifted).at[2:2 + 2 * twos:2].set(sink + shifted)
    return lengths[jax.random.permutation(jax.random.fold_in(key, 2), amount)]


def gaussian(key, shape, deviation, bound, pieces=(), kind=jnp.bfloat16):
    values = deviation * jax.random.normal(key, shape, jnp.float32)
    if pieces:
        values = values * block_levels(key, shape, pieces, -0.22, 0.18)
    return jnp.clip(values, -bound, bound).astype(kind)


def setup_inputs(seed: int = 0) -> dict:
    seeds = jax.random.split(jax.random.key(seed), 11)
    return {
        "y_first": gaussian(seeds[0], (TOKENS, D), 1.0, 6.0, ((0, 32), (1, 4))),
        "x_second": gaussian(seeds[1], (TOKENS, D), 1.0, 6.0, ((0, 32), (1, 4))),
        "grad_first": gaussian(seeds[2], (TOKENS, D), 1.0, 6.0, ((0, 32), (1, 4))),
        "grad_second": gaussian(seeds[3], (TOKENS, D), 1.0, 6.0, ((0, 32), (1, 4))),
        "doc_ids": jnp.searchsorted(jnp.cumsum(ragged_sizes(seeds[4], DOCS, TOKENS, TOKENS // 2, 2)), jnp.arange(TOKENS), side="right").astype(jnp.int32),
        "norm_gain": jnp.clip(1.0 + 0.15 * jax.random.normal(seeds[5], (D,), jnp.float32), 0.25, 1.75),
        "w_query": draw_w_query(jax.random.fold_in(seeds[10], 71), 0),
        "w_key": draw_w_key(jax.random.fold_in(seeds[10], 71), 0),
        "w_value": gaussian(seeds[8], (D, KV_HEADS * HEAD_DIM), D ** -0.5, 0.09375, ((1, 4),)),
        "w_out": gaussian(seeds[9], (HEADS * HEAD_DIM, D), (HEADS * HEAD_DIM // 4) ** -0.5, 0.25, ((0, 4),)),
    }


EPSILON = 1e-05
NEGATIVE = -1e+30

def rounded(values):
    return lax.optimization_barrier(values.astype(jnp.bfloat16)).astype(jnp.float32)

def reference(y_first, x_second, grad_first, grad_second, doc_ids, norm_gain, w_query, w_key, w_value, w_out):
    group_size = HEADS // KV_HEADS
    score_scale = HEAD_DIM ** (-0.5)
    inputs = x_second.astype(jnp.float32)
    inverse_rms = lax.rsqrt(lax.optimization_barrier(jnp.mean(inputs * inputs, axis=-1, keepdims=True)) + EPSILON)
    unit_rows = inputs * inverse_rms
    normed = (unit_rows * norm_gain).astype(jnp.bfloat16)
    queries = jnp.dot(normed, w_query, preferred_element_type=jnp.float32).astype(jnp.bfloat16)
    queries = queries.reshape(TOKENS, KV_HEADS, group_size, HEAD_DIM)
    key_rows = jnp.dot(normed, w_key, preferred_element_type=jnp.float32).astype(jnp.bfloat16)
    key_rows = key_rows.reshape(TOKENS, KV_HEADS, HEAD_DIM).astype(jnp.float32)
    value_rows = jnp.dot(normed, w_value, preferred_element_type=jnp.float32).astype(jnp.bfloat16)
    value_rows = value_rows.reshape(TOKENS, KV_HEADS, HEAD_DIM).astype(jnp.float32)
    positions = jnp.arange(TOKENS, dtype=jnp.int32)
    block_rows = min(512, TOKENS)
    block_count = TOKENS // block_rows
    starts = jnp.arange(block_count, dtype=jnp.int32) * block_rows

    def scores_of(first_row):
        query_block = lax.dynamic_slice_in_dim(queries, first_row, block_rows, 0).astype(jnp.float32)
        query_pos = first_row + jnp.arange(block_rows, dtype=jnp.int32)
        query_doc = lax.dynamic_slice_in_dim(doc_ids, first_row, block_rows, 0)
        allowed = (positions[None, :] <= query_pos[:, None]) & (doc_ids[None, :] == query_doc[:, None])
        scores = jnp.einsum('bkgd,tkd->bkgt', query_block, key_rows) * score_scale
        return (query_block, allowed[:, None, None, :], scores)

    def forward_block(first_row):
        query_block, allowed, scores = scores_of(first_row)
        row_max = lax.optimization_barrier(jnp.max(jnp.where(allowed, scores, NEGATIVE), axis=-1))
        weights = jnp.where(allowed, jnp.exp(scores - row_max[..., None]), 0.0)
        row_total = lax.optimization_barrier(jnp.sum(weights, axis=-1))
        log_total = row_max + jnp.log(row_total)
        probs = weights / row_total[..., None]
        mixed = jnp.einsum('bkgt,tkd->bkgd', probs, value_rows, precision=lax.Precision.HIGHEST).astype(jnp.bfloat16)
        return (mixed, log_total)
    attended, log_totals = lax.map(forward_block, starts)
    attended = attended.reshape(TOKENS, KV_HEADS, group_size, HEAD_DIM)
    log_totals = log_totals.reshape(TOKENS, KV_HEADS, group_size)
    branch = jnp.dot(attended.reshape(TOKENS, HEADS * HEAD_DIM), w_out, preferred_element_type=jnp.float32)
    x_first = y_first.astype(jnp.float32) - branch
    grad_attended = jnp.dot(grad_first, w_out.T, preferred_element_type=jnp.float32).astype(jnp.bfloat16)
    grad_attended = grad_attended.reshape(TOKENS, KV_HEADS, group_size, HEAD_DIM)
    deltas = lax.optimization_barrier(jnp.sum(grad_attended.astype(jnp.float32) * attended.astype(jnp.float32), axis=-1))

    def backward_block(carried, first_row):
        key_grad, value_grad = carried
        query_block, allowed, scores = scores_of(first_row)
        block_lse = lax.dynamic_slice_in_dim(log_totals, first_row, block_rows, 0)
        block_delta = lax.dynamic_slice_in_dim(deltas, first_row, block_rows, 0)
        block_grad = lax.dynamic_slice_in_dim(grad_attended, first_row, block_rows, 0).astype(jnp.float32)
        probs = jnp.where(allowed, jnp.exp(scores - block_lse[..., None]), 0.0)
        prob_grad = jnp.einsum('bkgd,tkd->bkgt', block_grad, value_rows)
        score_grad = rounded(probs * (prob_grad - block_delta[..., None]))
        query_grad = (score_scale * jnp.einsum('bkgt,tkd->bkgd', score_grad, key_rows)).astype(jnp.bfloat16)
        key_grad = key_grad + score_scale * jnp.einsum('bkgt,bkgd->tkd', score_grad, query_block)
        value_grad = value_grad + jnp.einsum('bkgt,bkgd->tkd', rounded(probs), block_grad)
        return ((key_grad, value_grad), query_grad)
    zero_grads = jnp.zeros((TOKENS, KV_HEADS, HEAD_DIM), jnp.float32)
    (key_grad, value_grad), query_grads = lax.scan(backward_block, (zero_grads, zero_grads), starts)
    query_grads = query_grads.reshape(TOKENS, HEADS * HEAD_DIM)
    key_grad = key_grad.astype(jnp.bfloat16).reshape(TOKENS, KV_HEADS * HEAD_DIM)
    value_grad = value_grad.astype(jnp.bfloat16).reshape(TOKENS, KV_HEADS * HEAD_DIM)
    normed_grad = jnp.dot(query_grads, w_query.T, preferred_element_type=jnp.float32)
    normed_grad = normed_grad + jnp.dot(key_grad, w_key.T, preferred_element_type=jnp.float32)
    normed_grad = normed_grad + jnp.dot(value_grad, w_value.T, preferred_element_type=jnp.float32)
    scaled = normed_grad * norm_gain
    input_grad = inverse_rms * (scaled - unit_rows * lax.optimization_barrier(jnp.mean(scaled * unit_rows, axis=-1, keepdims=True)))
    x_grad = grad_second.astype(jnp.float32) + input_grad
    return (x_first, x_grad)
```

```python
import jax
import jax.numpy as jnp
from jax import lax
from jax.experimental import pallas as pl
from jax.experimental.pallas import tpu as pltpu
from jax.sharding import PartitionSpec as P

HEAD = 128
EPSILON = 1e-05
MASKED = -1e30
SCALE = HEAD**-0.5
LOG2E = 1.4426950408889634
TOK = 256
HALF = TOK // 2
COLS = 1024
WIDTH = 4096
BAND = 17
ROWS_KV = TOK + 16
MIB = 1 << 20
NT = (((1,), (1,)), ((), ()))
TN = (((0,), (0,)), ((), ()))
F32 = jnp.float32
BF16 = jnp.bfloat16


def place():
    seq, mp = lax.axis_index("seq"), lax.axis_index("mp")
    core = lax.rem(seq, 2)
    x = lax.rem(lax.div(seq, 2), 4)
    y = lax.div(seq, 8)
    return seq, mp, y, x, core


def seq_of(y, x, core):
    return y * 8 + x * 2 + core


def plus(a, b, n=4):
    return lax.rem(a + (b + n) % n, n)


def remote(src, dst, sems, index, device):
    send, recv = sems
    return pltpu.make_async_remote_copy(
        src_ref=src,
        dst_ref=dst,
        send_sem=send.at[index],
        recv_sem=recv.at[index],
        device_id=device,
        device_id_type=pl.DeviceIdType.MESH,
    )


def greet(devices):
    barrier = pltpu.get_barrier_semaphore()
    for device in devices:
        pl.semaphore_signal(barrier, inc=1, device_id=device, device_id_type=pl.DeviceIdType.MESH)
    pl.semaphore_wait(barrier, len(devices))


class RingGather:
    def __init__(self, own, buf, slots, half, rows, sems, base, right, left):
        self.sems, self.base = sems, base
        me, l, r, o = slots
        a, b = pl.ds(0, half), pl.ds(half, rows - half)
        at = lambda slot, part: buf.at[slot, part]
        mk = lambda src, dst, i, dev: remote(src, dst, sems, base + i, dev)
        self.out = [
            mk(own.at[a], at(me, a), 0, right),
            mk(own.at[b], at(me, b), 1, right),
            mk(own.at[b], at(me, b), 2, left),
            mk(own.at[a], at(me, a), 3, left),
            mk(at(l, a), at(l, a), 4, right),
            mk(at(r, b), at(r, b), 5, left),
        ]
        self.inn = [
            mk(own.at[a], at(l, a), 0, right),
            mk(own.at[b], at(l, b), 1, right),
            mk(own.at[b], at(r, b), 2, left),
            mk(own.at[a], at(r, a), 3, left),
            mk(own.at[a], at(o, a), 4, right),
            mk(own.at[b], at(o, b), 5, left),
        ]

    def start(self):
        for i in (0, 2, 1, 3):
            self.out[i].start()

    def forward(self):
        self.inn[0].wait_recv()
        self.out[4].start()
        self.inn[2].wait_recv()
        self.out[5].start()

    def wait_left(self):
        self.inn[1].wait_recv()

    def wait_right(self):
        self.inn[3].wait_recv()

    def wait_far(self):
        self.inn[4].wait_recv()
        self.inn[5].wait_recv()

    def finish(self):
        for copy in self.out:
            copy.wait_send()


class RingReduce:
    def __init__(self, parts, relay, finals, slots, half, rows, sems, base, right, left):
        me, l, r, o = slots
        a, b = pl.ds(0, half), pl.ds(half, rows - half)
        self.parts, self.relay, self.finals = parts, relay, finals
        self.slots, self.a, self.b = slots, a, b
        mk = lambda src, dst, i, dev: remote(src, dst, sems, base + i, dev)
        self.out = [
            mk(parts(o, a), relay.at[0], 0, right),
            mk(parts(o, b), relay.at[1], 1, left),
            mk(parts(r, b), finals.at[0, b], 2, right),
            mk(parts(l, a), finals.at[1, a], 3, left),
            mk(parts(r, a), finals.at[0, a], 4, right),
            mk(parts(l, b), finals.at[1, b], 5, left),
        ]

    def start_far(self):
        self.out[0].start()
        self.out[1].start()

    def start_near(self):
        self.out[2].start()
        self.out[3].start()

    def forward(self):
        me, l, r, o = self.slots
        for i, slot, part in ((0, r, self.a), (1, l, self.b)):
            self.out[i].wait_recv()
            piece = self.parts(slot, part)
            piece[...] = (piece[...].astype(F32) + self.relay[i].astype(F32)).astype(BF16)
            self.out[4 + i].start()

    def wait_total(self):
        for i in (2, 3, 4, 5):
            self.out[i].wait_recv()
        me = self.slots[0]
        return lambda part: (
            self.parts(me, part)[...].astype(F32)
            + self.finals[0, part].astype(F32)
            + self.finals[1, part].astype(F32)
        )

    def finish(self):
        for copy in self.out:
            copy.wait_send()


def z_places(seq, mp):
    right, left, far = plus(mp, 1), plus(mp, -1), plus(mp, 2)
    return (mp, left, right, far), (seq, right), (seq, left), (seq, far)


def project_kernel(x_ref, gain_ref, docs_ref, wq_ref, wk_ref, wv_ref, q_ref, kvd_ref, inv_ref,
                   buf, weights, acc, scaled, mine, theirs, wsem, send, recv):
    seq, mp, y, x, core = place()
    slots, right, left, far = z_places(seq, mp)
    me, l, r, o = slots
    loads = []
    for n, slot in enumerate((me, l, r, o)):
        rows = pl.ds(pl.multiple_of(slot * COLS, COLS), COLS)
        group = []
        for i, (w, lo, hi) in enumerate(((wq_ref, 0, 512), (wk_ref, 512, 640), (wv_ref, 640, 768))):
            copy = pltpu.make_async_copy(w.at[rows], weights.at[rows, pl.ds(lo, hi - lo)], wsem.at[n, i])
            copy.start()
            group.append(copy)
        loads.append(group)
    values = x_ref[...].astype(F32)
    squares = jnp.sum(values * values, axis=-1, keepdims=True)
    mine[...] = jnp.broadcast_to(squares, (TOK, 128)).T[0:8, :]
    sems = (send, recv)
    greet([right, left, far])
    small = [
        remote(mine, theirs.at[i], sems, 6 + i, device) for i, device in enumerate((right, left, far))
    ]
    for copy in small:
        copy.start()
    ring = RingGather(x_ref, buf, slots, HALF, TOK, sems, 0, right, left)
    ring.start()
    kvd_ref[pl.ds(TOK, 16), :] = docs_ref[...]
    for copy in small:
        copy.wait_recv()
    squares = mine[...] + theirs[0] + theirs[1] + theirs[2]
    inverse = lax.rsqrt(squares[0:1, :] * (1.0 / WIDTH) + EPSILON)
    inv_ref[...] = jnp.broadcast_to(inverse, (128, TOK)).T

    def fold(n, slot, block):
        for copy in loads[n]:
            copy.wait()
        scaled[...] = (block[...].astype(F32) * inv_ref[:, 0:1] * gain_ref[pl.ds(slot, 1), :]).astype(BF16)
        rows = pl.ds(pl.multiple_of(slot * COLS, COLS), COLS)

        def column(i, carry):
            cols = pl.ds(pl.multiple_of(i * 256, 256), 256)
            term = jnp.dot(scaled[...], weights[rows, cols], preferred_element_type=F32)
            if n == 0:
                acc[:, cols] = term
            else:
                acc[:, cols] += term
            return carry

        lax.fori_loop(0, 3, column, 0)

    fold(0, me, x_ref)
    ring.forward()
    ring.wait_left()
    fold(1, l, buf.at[l])
    ring.wait_right()
    fold(2, r, buf.at[r])
    ring.wait_far()
    fold(3, o, buf.at[o])
    q_ref[...] = acc[:, pl.ds(0, 512)].astype(BF16)
    kvd_ref[pl.ds(0, TOK), :] = acc[:, pl.ds(512, 256)].astype(BF16)
    for copy in small:
        copy.wait_send()
    ring.finish()


VM = pl.BlockSpec(memory_space=pltpu.VMEM)
ANY = pl.BlockSpec(memory_space=pl.ANY)
DMA = pltpu.SemaphoreType.DMA


def project(x, gain, docs, w_query, w_key, w_value):
    return pl.pallas_call(
        project_kernel,
        name="project",
        out_shape=(
            jax.ShapeDtypeStruct((TOK, 512), BF16),
            jax.ShapeDtypeStruct((ROWS_KV, 256), BF16),
            jax.ShapeDtypeStruct((TOK, 128), F32),
        ),
        in_specs=[VM, VM, VM, ANY, ANY, ANY],
        out_specs=(VM, VM, VM),
        scratch_shapes=[
            pltpu.VMEM((4, TOK, COLS), BF16),
            pltpu.VMEM((WIDTH, 768), BF16),
            pltpu.VMEM((TOK, 768), F32),
            pltpu.VMEM((TOK, COLS), BF16),
            pltpu.VMEM((8, TOK), F32),
            pltpu.VMEM((3, 8, TOK), F32),
            DMA((4, 3)),
            DMA((9,)),
            DMA((9,)),
        ],
        compiler_params=pltpu.CompilerParams(
            collective_id=0, has_side_effects=True, vmem_limit_bytes=24 * MIB
        ),
    )(x, gain, docs, w_query, w_key, w_value)


def band_kernel(kvd_ref, g_ref, w_ref, kvb_ref, go_ref, buf, weights, acc, wsem, osem,
                zsend, zrecv, send, recv):
    seq, mp, y, x, core = place()
    slots, zright, zleft, zfar = z_places(seq, mp)
    me, l, r, o = slots
    loads = []
    for n, slot in enumerate((me, l, r, o)):
        cols = pl.ds(pl.multiple_of(slot * COLS, COLS), COLS)
        copy = pltpu.make_async_copy(w_ref.at[:, cols], weights.at[slot], wsem.at[n])
        copy.start()
        loads.append(copy)
    xr, xl, xo = plus(x, 1), plus(x, -1), plus(x, 2)
    up, down = (seq_of(plus(y, 1), x, core), mp), (seq_of(plus(y, -1), x, core), mp)
    right, left = (seq_of(y, xr, core), mp), (seq_of(y, xl, core), mp)
    partner = (seq_of(y, x, 1 - core), mp)
    own_copy = pltpu.make_async_copy(kvd_ref, kvb_ref.at[seq], osem.at[0])
    own_copy.start()
    greet([up, down, right, left, partner, zright, zleft])
    sems = (send, recv)
    zring = RingGather(g_ref, buf, slots, HALF, TOK, (zsend, zrecv), 0, zright, zleft)
    rows = [plus(y, -k) for k in range(3)]
    rings, across, across_in = [], [], []
    for k in range(3):
        at = [seq_of(rows[k], column, core) for column in (x, xl, xr, xo)]
        own = kvd_ref if k == 0 else kvb_ref.at[at[0]]
        rings.append(RingGather(own, kvb_ref, at, 128, ROWS_KV, sems, 6 * k, right, left))
        twin = [seq_of(rows[k], column, 1 - core) for column in (x, xl, xr, xo)]
        out, inn = [], []
        for n in range(4):
            src = kvd_ref if k == 0 and n == 0 else kvb_ref.at[at[n]]
            out.append(remote(src, kvb_ref.at[at[n]], sems, 18 + 4 * k + n, partner))
            inn.append(remote(src, kvb_ref.at[twin[n]], sems, 18 + 4 * k + n, partner))
        across.append(out)
        across_in.append(inn)
    b1, b2 = seq_of(rows[1], x, core), seq_of(rows[2], x, core)
    up_own = remote(kvd_ref, kvb_ref.at[seq], sems, 30, up)
    in_own = remote(kvd_ref, kvb_ref.at[b1], sems, 30, up)
    up_next = remote(kvb_ref.at[b1], kvb_ref.at[b1], sems, 31, up)
    in_next = remote(kvb_ref.at[b1], kvb_ref.at[b2], sems, 31, up)

    up_own.start()
    rings[0].start()
    zring.start()
    across[0][0].start()

    def fold(n, slot, block):
        loads[n].wait()
        term = lax.dot_general(block[...], weights[slot], NT, preferred_element_type=F32)
        if n == 0:
            acc[...] = term
        else:
            acc[...] += term

    rings[0].forward()
    in_own.wait_recv()
    up_next.start()
    rings[1].start()
    across[1][0].start()
    fold(0, me, g_ref)
    in_next.wait_recv()
    rings[2].start()
    across[2][0].start()
    rings[1].forward()
    zring.forward()
    for k in range(3):
        if k == 2:
            rings[2].forward()
        rings[k].wait_left()
        across[k][1].start()
        rings[k].wait_right()
        across[k][2].start()
    zring.wait_left()
    fold(1, l, buf.at[l])
    zring.wait_right()
    fold(2, r, buf.at[r])
    for k in range(3):
        rings[k].wait_far()
        across[k][3].start()
    zring.wait_far()
    fold(3, o, buf.at[o])
    go_ref[...] = acc[...].astype(BF16)
    own_copy.wait()
    for k in range(3):
        for n in range(4):
            across_in[k][n].wait_recv()
    up_own.wait_send()
    up_next.wait_send()
    zring.finish()
    for k in range(3):
        rings[k].finish()
        for n in range(4):
            across[k][n].wait_send()


def band(kvd, g, w_out):
    return pl.pallas_call(
        band_kernel,
        name="band",
        out_shape=(
            jax.ShapeDtypeStruct((32, ROWS_KV, 256), BF16),
            jax.ShapeDtypeStruct((TOK, 512), BF16),
        ),
        in_specs=[VM, VM, ANY],
        out_specs=(VM, VM),
        scratch_shapes=[
            pltpu.VMEM((4, TOK, COLS), BF16),
            pltpu.VMEM((4, 512, COLS), BF16),
            pltpu.VMEM((TOK, 512), F32),
            DMA((4,)),
            DMA((1,)),
            DMA((6,)),
            DMA((6,)),
            DMA((32,)),
            DMA((32,)),
        ],
        compiler_params=pltpu.CompilerParams(
            collective_id=1, has_side_effects=True, vmem_limit_bytes=24 * MIB
        ),
    )(kvd, g, w_out)


def attention_kernel(q_ref, kvb_ref, go_ref, docs_ref, att_ref, dq_ref, dkv_ref,
                     s_buf, p_buf, ka_buf, qt, qs, dot_buf, do_buf, o_acc, dq_acc, m_buf, l_buf, li_buf):
    seq = lax.axis_index("seq")
    blocks = jnp.minimum(seq, BAND - 1) + 1
    heads = [pl.ds(h * TOK, TOK) for h in range(4)]

    def clear(i, carry):
        dkv_ref[i] = jnp.zeros((TOK, 256), BF16)
        return carry

    lax.fori_loop(0, 32, clear, 0)
    for h in range(4):
        piece = q_ref[:, pl.ds(h * HEAD, HEAD)]
        qs[heads[h], :] = piece
        qt[pl.ds(0, HEAD), heads[h]] = piece.astype(F32).T.astype(BF16)
    docs = docs_ref[pl.ds(0, 8), :].astype(F32)[0:1, :]
    number = lax.broadcasted_iota(jnp.int32, (HEAD, TOK), 0).astype(F32)
    other = jnp.where(number == docs, 0.0, MASKED).astype(BF16)
    for h in range(4):
        qt[pl.ds(HEAD, HEAD), heads[h]] = other
    m_buf[...] = jnp.full(m_buf.shape, MASKED, F32)
    l_buf[...] = jnp.zeros(l_buf.shape, F32)
    o_acc[...] = jnp.zeros(o_acc.shape, F32)
    dq_acc[...] = jnp.zeros(dq_acc.shape, F32)

    def score(j, diagonal):
        b = seq - j
        key_docs = kvb_ref[b, pl.ds(TOK, 16), :].astype(F32)[0:1, :]
        same = jnp.where(number == key_docs, 1.0, 0.0)
        ka_buf[j, :, pl.ds(0, HEAD)] = kvb_ref[b, pl.ds(0, TOK), pl.ds(0, HEAD)]
        ka_buf[j, :, pl.ds(HEAD, HEAD)] = same.T.astype(BF16)
        for h in range(4):
            s = jnp.dot(ka_buf[j], qt[:, heads[h]], preferred_element_type=F32)
            if diagonal:
                key_at = lax.broadcasted_iota(jnp.int32, (TOK, TOK), 0)
                query_at = lax.broadcasted_iota(jnp.int32, (TOK, TOK), 1)
                s = jnp.where(key_at <= query_at, s, MASKED)
            s_buf[j, :, heads[h]] = s
            m_buf[:, heads[h]] = jnp.maximum(m_buf[:, heads[h]], s.reshape(TOK // 8, 8, TOK).max(axis=0))

    score(0, True)

    def score_step(j, carry):
        score(j, False)
        return carry

    lax.fori_loop(1, blocks, score_step, 0)
    top = jnp.max(m_buf[...], axis=0, keepdims=True)
    m_buf[...] = jnp.broadcast_to(top, m_buf.shape)

    def mix_step(j, carry):
        b = seq - j
        values = kvb_ref[b, pl.ds(0, TOK), pl.ds(HEAD, HEAD)]
        for h in range(4):
            s = s_buf[j, :, heads[h]]
            p = jnp.exp2((s - m_buf[0:1, heads[h]]) * (SCALE * LOG2E))
            l_buf[:, heads[h]] += p.reshape(TOK // 8, 8, TOK).sum(axis=0)
            p_buf[j, :, heads[h]] = p.astype(BF16)
            o_acc[:, heads[h]] += lax.dot_general(
                values, p.astype(BF16), TN, preferred_element_type=F32
            )
        return carry

    lax.fori_loop(0, blocks, mix_step, 0)
    inverse = 1.0 / jnp.sum(l_buf[...], axis=0, keepdims=True)
    li_buf[...] = jnp.broadcast_to(inverse, (8, 1024))
    for h in range(4):
        mixed = (o_acc[:, heads[h]] * inverse[:, h * TOK : (h + 1) * TOK]).astype(BF16).astype(F32)
        att_ref[:, pl.ds(h * HEAD, HEAD)] = mixed.T.astype(BF16)
        grad = go_ref[:, pl.ds(h * HEAD, HEAD)].astype(F32).T
        dot_buf[:, heads[h]] = grad.astype(BF16)
        do_buf[heads[h], :] = grad.T.astype(BF16)
        l_buf[:, heads[h]] = jnp.broadcast_to(jnp.sum(grad * mixed, axis=0, keepdims=True), (8, TOK))

    def back_step(j, carry):
        b = seq - j
        values = kvb_ref[b, pl.ds(0, TOK), pl.ds(HEAD, HEAD)]
        keys = kvb_ref[b, pl.ds(0, TOK), pl.ds(0, HEAD)]
        key_grad = jnp.zeros((TOK, HEAD), F32)
        value_grad = jnp.zeros((TOK, HEAD), F32)
        for h in range(4):
            s = s_buf[j, :, heads[h]]
            pf = jnp.exp2((s - m_buf[0:1, heads[h]]) * (SCALE * LOG2E)) * li_buf[0:1, heads[h]]
            p = pf.astype(BF16)
            dp = jnp.dot(values, dot_buf[:, heads[h]], preferred_element_type=F32)
            ds = (pf * (dp - l_buf[0:1, heads[h]])).astype(BF16)
            value_grad += jnp.dot(p, do_buf[heads[h], :], preferred_element_type=F32)
            key_grad += jnp.dot(ds, qs[heads[h], :], preferred_element_type=F32)
            dq_acc[:, heads[h]] += lax.dot_general(keys, ds, TN, preferred_element_type=F32)
        dkv_ref[b, :, pl.ds(0, HEAD)] = (key_grad * SCALE).astype(BF16)
        dkv_ref[b, :, pl.ds(HEAD, HEAD)] = value_grad.astype(BF16)
        return carry

    lax.fori_loop(0, blocks, back_step, 0)
    for h in range(4):
        dq_ref[:, pl.ds(h * HEAD, HEAD)] = (dq_acc[:, heads[h]] * SCALE).T.astype(BF16)


def attention(q, kvb, go, docs):
    return pl.pallas_call(
        attention_kernel,
        name="attention",
        out_shape=(
            jax.ShapeDtypeStruct((TOK, 512), BF16),
            jax.ShapeDtypeStruct((TOK, 512), BF16),
            jax.ShapeDtypeStruct((32, TOK, 256), BF16),
        ),
        in_specs=[VM] * 4,
        out_specs=(VM, VM, VM),
        scratch_shapes=[
            pltpu.VMEM((BAND, TOK, 1024), F32),
            pltpu.VMEM((BAND, TOK, 1024), BF16),
            pltpu.VMEM((BAND, TOK, 256), BF16),
            pltpu.VMEM((256, 1024), BF16),
            pltpu.VMEM((1024, HEAD), BF16),
            pltpu.VMEM((HEAD, 1024), BF16),
            pltpu.VMEM((1024, HEAD), BF16),
            pltpu.VMEM((HEAD, 1024), F32),
            pltpu.VMEM((HEAD, 1024), F32),
            pltpu.VMEM((8, 1024), F32),
            pltpu.VMEM((8, 1024), F32),
            pltpu.VMEM((8, 1024), F32),
        ],
        compiler_params=pltpu.CompilerParams(vmem_limit_bytes=56 * MIB),
    )(q, kvb, go, docs)


def collect_kernel(dkv_ref, att_ref, w_ref, grad_ref, branch_ref,
                   twin, sums, xrelay, xfinal, ynear, yown, weights, parts, zrelay, zfinal,
                   wsem, send, recv, zsend, zrecv):
    seq, mp, y, x, core = place()
    slots, zright, zleft, zfar = z_places(seq, mp)
    me, l, r, o = slots
    loads = []
    for n, slot in enumerate((o, r, l, me)):
        cols = pl.ds(pl.multiple_of(slot * COLS, COLS), COLS)
        copy = pltpu.make_async_copy(w_ref.at[:, cols], weights.at[slot], wsem.at[n])
        copy.start()
        loads.append(copy)
    xr, xl, xo = plus(x, 1), plus(x, -1), plus(x, 2)
    up, down = (seq_of(plus(y, 1), x, core), mp), (seq_of(plus(y, -1), x, core), mp)
    right, left = (seq_of(y, xr, core), mp), (seq_of(y, xl, core), mp)
    partner = (seq_of(y, x, 1 - core), mp)
    greet([up, down, right, left, partner, zright, zleft])
    sems = (send, recv)
    order = (2, 1, 0)
    rows = [plus(y, -k) for k in range(3)]
    across = [
        remote(dkv_ref.at[rows[k], :, 1 - core], twin.at[k], sems, k, partner) for k in range(3)
    ]
    for k in order:
        across[k].start()

    def term(n, slot):
        loads[n].wait()
        parts[slot] = jnp.dot(att_ref[...], weights[slot], preferred_element_type=F32).astype(BF16)

    zring = RingReduce(
        lambda slot, part: parts.at[slot, part], zrelay, zfinal, slots, HALF, TOK,
        (zsend, zrecv), 0, zright, zleft,
    )
    term(0, o)
    zring.start_far()
    rings = []
    for k in range(3):
        rings.append(
            RingReduce(
                lambda slot, part, k=k: sums.at[k, slot, part],
                xrelay.at[k], xfinal.at[k], (x, xl, xr, xo), HALF, TOK, sems, 3 + 6 * k, right, left,
            )
        )

    def open_ring(k):
        across[k].wait_recv()

        def add(i, carry):
            mine = dkv_ref[rows[k], i, core].astype(F32)
            sums[k, i] = (mine + twin[k, i].astype(F32)).astype(BF16)
            return carry

        lax.fori_loop(0, 4, add, 0)
        rings[k].start_far()
        rings[k].start_near()

    whole = pl.ds(0, TOK)
    open_ring(2)
    term(1, r)
    term(2, l)
    zring.start_near()
    open_ring(1)
    rings[2].forward()
    open_ring(0)
    rings[1].forward()
    term(3, me)
    far_up = remote(yown.at[0], ynear.at[0], sems, 21, down)
    near_up = remote(yown.at[1], ynear.at[1], sems, 22, down)
    zring.forward()
    yown[0] = rings[2].wait_total()(whole).astype(BF16)
    far_up.start()
    rings[0].forward()
    total = rings[1].wait_total()(whole)
    far_up.wait_recv()
    yown[1] = (total + ynear[0].astype(F32)).astype(BF16)
    near_up.start()
    total = rings[0].wait_total()(whole)
    near_up.wait_recv()
    grad_ref[...] = (total + ynear[1].astype(F32)).astype(BF16)
    total = zring.wait_total()
    for part in (pl.ds(0, HALF), pl.ds(HALF, HALF)):
        branch_ref[part, :] = total(part)
    for copy in across + [far_up, near_up]:
        copy.wait_send()
    for ring in rings + [zring]:
        ring.finish()


def collect(dkv, att, w_out):
    return pl.pallas_call(
        collect_kernel,
        name="collect",
        out_shape=(
            jax.ShapeDtypeStruct((TOK, 256), BF16),
            jax.ShapeDtypeStruct((TOK, COLS), F32),
        ),
        in_specs=[VM, VM, ANY],
        out_specs=(VM, VM),
        scratch_shapes=[
            pltpu.VMEM((3, 4, TOK, 256), BF16),
            pltpu.VMEM((3, 4, TOK, 256), BF16),
            pltpu.VMEM((3, 2, HALF, 256), BF16),
            pltpu.VMEM((3, 2, TOK, 256), BF16),
            pltpu.VMEM((2, TOK, 256), BF16),
            pltpu.VMEM((2, TOK, 256), BF16),
            pltpu.VMEM((4, 512, COLS), BF16),
            pltpu.VMEM((4, TOK, COLS), BF16),
            pltpu.VMEM((2, HALF, COLS), BF16),
            pltpu.VMEM((2, TOK, COLS), BF16),
            DMA((4,)),
            DMA((23,)),
            DMA((23,)),
            DMA((6,)),
            DMA((6,)),
        ],
        compiler_params=pltpu.CompilerParams(
            collective_id=2, has_side_effects=True, vmem_limit_bytes=32 * MIB
        ),
    )(dkv, att, w_out)


def norm_kernel(q_ref, kvd_ref, dq_ref, dkv_ref, wq_ref, wk_ref, wv_ref, out_ref, dot_ref,
                weights, grads, parts, relay, final, mine, theirs, wsem, send, recv):
    seq, mp, y, x, core = place()
    slots, right, left, far = z_places(seq, mp)
    me, l, r, o = slots
    loads = []
    for n, slot in enumerate((o, r, l, me)):
        rows = pl.ds(pl.multiple_of(slot * COLS, COLS), COLS)
        group = []
        for i, (w, lo, hi) in enumerate(((wq_ref, 0, 512), (wk_ref, 512, 640), (wv_ref, 640, 768))):
            copy = pltpu.make_async_copy(w.at[rows], weights.at[rows, pl.ds(lo, hi - lo)], wsem.at[n, i])
            copy.start()
            group.append(copy)
        loads.append(group)
    grads[:, pl.ds(0, 512)] = dq_ref[...]
    grads[:, pl.ds(512, 256)] = dkv_ref[...]
    greet([right, left, far])
    sems = (send, recv)

    def term(n, slot):
        for copy in loads[n]:
            copy.wait()

        def column(i, carry):
            rows = pl.ds(pl.multiple_of(slot * COLS + i * 256, 256), 256)
            cols = pl.ds(pl.multiple_of(i * 256, 256), 256)
            piece = lax.dot_general(grads[...], weights[rows, :], NT, preferred_element_type=F32)
            parts[slot, :, cols] = piece.astype(BF16)
            return carry

        lax.fori_loop(0, 4, column, 0)

    ring = RingReduce(
        lambda slot, part: parts.at[slot, part], relay, final, slots, HALF, TOK, sems, 0, right, left
    )
    term(0, o)
    ring.start_far()
    term(1, r)
    term(2, l)
    ring.start_near()
    dots = jnp.sum(q_ref[...].astype(F32) * dq_ref[...].astype(F32), axis=-1, keepdims=True)
    dots += jnp.sum(
        kvd_ref[pl.ds(0, TOK), :].astype(F32) * dkv_ref[...].astype(F32), axis=-1, keepdims=True
    )
    mine[...] = jnp.broadcast_to(dots, (TOK, 128)).T[0:8, :]
    small = [
        remote(mine, theirs.at[i], sems, 6 + i, device) for i, device in enumerate((right, left, far))
    ]
    for copy in small:
        copy.start()
    term(3, me)
    ring.forward()
    for copy in small:
        copy.wait_recv()
    dot_ref[...] = mine[...] + theirs[0] + theirs[1] + theirs[2]
    total = ring.wait_total()
    for part in (pl.ds(0, HALF), pl.ds(HALF, HALF)):
        out_ref[part, :] = total(part)
    for copy in small:
        copy.wait_send()
    ring.finish()


def norm_grad(q, kvd, dq, dkv, w_query, w_key, w_value):
    return pl.pallas_call(
        norm_kernel,
        name="norm_grad",
        out_shape=(
            jax.ShapeDtypeStruct((TOK, COLS), F32),
            jax.ShapeDtypeStruct((8, TOK), F32),
        ),
        in_specs=[VM, VM, VM, VM, ANY, ANY, ANY],
        out_specs=(VM, VM),
        scratch_shapes=[
            pltpu.VMEM((WIDTH, 768), BF16),
            pltpu.VMEM((TOK, 768), BF16),
            pltpu.VMEM((4, TOK, COLS), BF16),
            pltpu.VMEM((2, HALF, COLS), BF16),
            pltpu.VMEM((2, TOK, COLS), BF16),
            pltpu.VMEM((8, TOK), F32),
            pltpu.VMEM((3, 8, TOK), F32),
            DMA((4, 3)),
            DMA((9,)),
            DMA((9,)),
        ],
        compiler_params=pltpu.CompilerParams(
            collective_id=3, has_side_effects=True, vmem_limit_bytes=24 * MIB
        ),
    )(q, kvd, dq, dkv, w_query, w_key, w_value)


def per_device(
    y_first, x_second, grad_first, grad_second, doc_ids, norm_gain, w_query, w_key, w_value, w_out
):
    mp = lax.axis_index("mp")
    docs = jnp.broadcast_to(doc_ids.astype(BF16)[None, :], (16, TOK))
    gains = norm_gain.reshape(4, COLS)
    q, kvd, inverse = project(x_second, gains, docs, w_query, w_key, w_value)
    kvb, go = band(kvd, grad_first, w_out)
    att, dq, dkv = attention(q, kvb, go, docs)
    dkv, branch = collect(dkv.reshape(4, 4, 2, TOK, 256), att, w_out)
    x_first = y_first.astype(F32) - branch
    shared, dots = norm_grad(q, kvd, dq, dkv, w_query, w_key, w_value)
    inverse = inverse[:, :1]
    unit = x_second.astype(F32) * inverse
    gain = lax.dynamic_slice_in_dim(gains, mp, 1, 0)
    mean = (dots[0] * (1.0 / WIDTH))[:, None]
    x_grad = grad_second.astype(F32) + inverse * (shared * gain - unit * mean)
    return (x_first, x_grad)


def solution(mesh):
    placed = (
        P("seq", "mp"),
        P("seq", "mp"),
        P("seq", "mp"),
        P("seq", "mp"),
        P("seq"),
        P(),
        P(None, "mp"),
        P(None, "mp"),
        P(None, "mp"),
        P("mp", None),
    )
    return jax.shard_map(
        per_device,
        mesh=mesh,
        in_specs=placed,
        out_specs=(P("seq", "mp"), P("seq", "mp")),
        check_vma=False,
    )
```

```python
import jax
import jax.numpy as jnp
from jax import lax
from jax.experimental import pallas as pl
from jax.experimental.pallas import tpu as pltpu
from jax.sharding import PartitionSpec as P

HEAD = 128
EPSILON = 1e-05
MASKED = -1e30
SCALE = HEAD**-0.5
LOG2E = 1.4426950408889634
TOK = 256
HALF = TOK // 2
COLS = 1024
WIDTH = 4096
BAND = 17
ROWS_KV = TOK + 16
MIB = 1 << 20
NT = (((1,), (1,)), ((), ()))
TN = (((0,), (0,)), ((), ()))
F32 = jnp.float32
BF16 = jnp.bfloat16


def place():
    seq, mp = lax.axis_index("seq"), lax.axis_index("mp")
    core = lax.rem(seq, 2)
    x = lax.rem(lax.div(seq, 2), 4)
    y = lax.div(seq, 8)
    return seq, mp, y, x, core


def seq_of(y, x, core):
    return y * 8 + x * 2 + core


def plus(a, b, n=4):
    return lax.rem(a + (b + n) % n, n)


def remote(src, dst, sems, index, device):
    send, recv = sems
    return pltpu.make_async_remote_copy(
        src_ref=src,
        dst_ref=dst,
        send_sem=send.at[index],
        recv_sem=recv.at[index],
        device_id=device,
        device_id_type=pl.DeviceIdType.MESH,
    )


def greet(devices):
    barrier = pltpu.get_barrier_semaphore()
    for device in devices:
        pl.semaphore_signal(barrier, inc=1, device_id=device, device_id_type=pl.DeviceIdType.MESH)
    pl.semaphore_wait(barrier, len(devices))


class RingGather:
    def __init__(self, own, buf, slots, half, rows, sems, base, right, left):
        self.sems, self.base = sems, base
        me, l, r, o = slots
        a, b = pl.ds(0, half), pl.ds(half, rows - half)
        at = lambda slot, part: buf.at[slot, part]
        mk = lambda src, dst, i, dev: remote(src, dst, sems, base + i, dev)
        self.out = [
            mk(own.at[a], at(me, a), 0, right),
            mk(own.at[b], at(me, b), 1, right),
            mk(own.at[b], at(me, b), 2, left),
            mk(own.at[a], at(me, a), 3, left),
            mk(at(l, a), at(l, a), 4, right),
            mk(at(r, b), at(r, b), 5, left),
        ]
        self.inn = [
            mk(own.at[a], at(l, a), 0, right),
            mk(own.at[b], at(l, b), 1, right),
            mk(own.at[b], at(r, b), 2, left),
            mk(own.at[a], at(r, a), 3, left),
            mk(own.at[a], at(o, a), 4, right),
            mk(own.at[b], at(o, b), 5, left),
        ]

    def start(self):
        for i in (0, 2, 1, 3):
            self.out[i].start()

    def forward(self):
        self.inn[0].wait_recv()
        self.out[4].start()
        self.inn[2].wait_recv()
        self.out[5].start()

    def wait_left(self):
        self.inn[1].wait_recv()

    def wait_right(self):
        self.inn[3].wait_recv()

    def wait_far(self):
        self.inn[4].wait_recv()
        self.inn[5].wait_recv()

    def finish(self):
        for copy in self.out:
            copy.wait_send()


class RingReduce:
    def __init__(self, parts, relay, finals, slots, half, rows, sems, base, right, left):
        me, l, r, o = slots
        a, b = pl.ds(0, half), pl.ds(half, rows - half)
        self.parts, self.relay, self.finals = parts, relay, finals
        self.slots, self.a, self.b = slots, a, b
        mk = lambda src, dst, i, dev: remote(src, dst, sems, base + i, dev)
        self.out = [
            mk(parts(o, a), relay.at[0], 0, right),
            mk(parts(o, b), relay.at[1], 1, left),
            mk(parts(r, b), finals.at[0, b], 2, right),
            mk(parts(l, a), finals.at[1, a], 3, left),
            mk(parts(r, a), finals.at[0, a], 4, right),
            mk(parts(l, b), finals.at[1, b], 5, left),
        ]

    def start_far(self):
        self.out[0].start()
        self.out[1].start()

    def start_near(self):
        self.out[2].start()
        self.out[3].start()

    def forward(self):
        me, l, r, o = self.slots
        for i, slot, part in ((0, r, self.a), (1, l, self.b)):
            self.out[i].wait_recv()
            piece = self.parts(slot, part)
            piece[...] = (piece[...].astype(F32) + self.relay[i].astype(F32)).astype(BF16)
            self.out[4 + i].start()

    def wait_total(self):
        for i in (2, 3, 4, 5):
            self.out[i].wait_recv()
        me = self.slots[0]
        return lambda part: (
            self.parts(me, part)[...].astype(F32)
            + self.finals[0, part].astype(F32)
            + self.finals[1, part].astype(F32)
        )

    def finish(self):
        for copy in self.out:
            copy.wait_send()


def z_places(seq, mp):
    right, left, far = plus(mp, 1), plus(mp, -1), plus(mp, 2)
    return (mp, left, right, far), (seq, right), (seq, left), (seq, far)


VM = pl.BlockSpec(memory_space=pltpu.VMEM)
ANY = pl.BlockSpec(memory_space=pl.ANY)
DMA = pltpu.SemaphoreType.DMA


def block_kernel(x_ref, g_ref, docs_ref, gain_ref, wq_ref, wk_ref, wv_ref, wo_ref,
                 branch_ref, out_ref, dot_ref, inv_ref,
                 x_buf, g_buf, weights, w_out, acc, go_acc, scaled, mine, theirs, kvb, s_buf, ka, qt, qs,
                 dot_buf, do_buf, o_acc, dq_acc, m_buf, m_run, l_buf, li_buf, d_buf, att, dkv, twin, sums,
                 xrelay, xfinal, ynear, yown, brelay, bfinal, nrelay, nfinal, grads,
                 lsem, zsend, zrecv, send, recv):
    seq, mp, y, x, core = place()
    slots, zright, zleft, zfar = z_places(seq, mp)
    me, l, r, o = slots
    zsems, sems = (zsend, zrecv), (send, recv)
    xr, xl, xo = plus(x, 1), plus(x, -1), plus(x, 2)
    up, down = (seq_of(plus(y, 1), x, core), mp), (seq_of(plus(y, -1), x, core), mp)
    right, left = (seq_of(y, xr, core), mp), (seq_of(y, xl, core), mp)
    partner = (seq_of(y, x, 1 - core), mp)
    rows = [plus(y, -k) for k in range(3)]
    heads = [pl.ds(h * TOK, TOK) for h in range(4)]
    whole = pl.ds(0, TOK)

    x_load = pltpu.make_async_copy(x_ref, x_buf.at[me], lsem.at[0])
    x_load.start()
    loads = []
    for n, slot in enumerate((me, l, r, o)):
        at = pl.ds(pl.multiple_of(slot * COLS, COLS), COLS)
        group = []
        for i, (w, lo, hi) in enumerate(((wq_ref, 0, 512), (wk_ref, 512, 640), (wv_ref, 640, 768))):
            copy = pltpu.make_async_copy(w.at[at], weights.at[at, pl.ds(lo, hi - lo)], lsem.at[1 + 3 * n + i])
            copy.start()
            group.append(copy)
        loads.append(group)
    g_load = pltpu.make_async_copy(g_ref, g_buf.at[me], lsem.at[13])
    g_load.start()
    w_loads = []
    for n, slot in enumerate((me, l, r, o)):
        cols = pl.ds(pl.multiple_of(slot * COLS, COLS), COLS)
        copy = pltpu.make_async_copy(wo_ref.at[:, cols], w_out.at[slot], lsem.at[14 + n])
        copy.start()
        w_loads.append(copy)

    x_load.wait()
    values = x_buf[me].astype(F32)
    squares = jnp.sum(values * values, axis=-1, keepdims=True)
    mine[0] = jnp.broadcast_to(squares, (TOK, 128)).T[0:8, :]
    greet([up, down, right, left, partner, zright, zleft, zfar])

    def exchange(which, base):
        return [
            remote(mine.at[which], theirs.at[which, i], zsems, base + i, device)
            for i, device in enumerate((zright, zleft, zfar))
        ]

    small = exchange(0, 6)
    for copy in small:
        copy.start()
    x_ring = RingGather(x_buf.at[me], x_buf, slots, HALF, TOK, zsems, 0, zright, zleft)
    x_ring.start()
    docs = docs_ref[...].astype(F32)
    kvb[seq, pl.ds(TOK, 16), :] = jnp.broadcast_to(docs, (16, TOK)).astype(BF16)

    def clear(i, carry):
        for k in range(3):
            for c in range(2):
                dkv[k, i, c] = jnp.zeros((TOK, 256), BF16)
        return carry

    lax.fori_loop(0, 4, clear, 0)
    for copy in small:
        copy.wait_recv()
    squares = mine[0] + theirs[0, 0] + theirs[0, 1] + theirs[0, 2]
    inverse = lax.rsqrt(squares[0:1, :] * (1.0 / WIDTH) + EPSILON)
    inv_ref[...] = jnp.broadcast_to(inverse, (128, TOK)).T

    def column(n, slot, i):
        at = pl.ds(pl.multiple_of(slot * COLS, COLS), COLS)
        cols = pl.ds(i * 256, 256)
        term = jnp.dot(scaled[...], weights[at, cols], preferred_element_type=F32)
        acc[:, cols] = term if n == 0 else acc[:, cols] + term

    def scale_rows(n, slot):
        for copy in loads[n]:
            copy.wait()
        gain = gain_ref[:, pl.ds(pl.multiple_of(slot * COLS, COLS), COLS)]
        scaled[...] = (x_buf[slot].astype(F32) * inv_ref[:, 0:1] * gain).astype(BF16)

    def fold(n, slot):
        scale_rows(n, slot)
        for i in range(3):
            column(n, slot, i)

    def fold_grad(n, slot):
        w_loads[n].wait()
        term = lax.dot_general(g_buf[slot], w_out[slot], NT, preferred_element_type=F32)
        go_acc[...] = term if n == 0 else go_acc[...] + term

    g_ring = RingGather(g_buf.at[me], g_buf, slots, HALF, TOK, zsems, 9, zright, zleft)
    fold(0, me)
    x_ring.forward()
    g_load.wait()
    g_ring.start()
    fold_grad(0, me)
    x_ring.wait_left()
    fold(1, l)
    x_ring.wait_right()
    fold(2, r)
    x_ring.wait_far()
    scale_rows(3, o)
    column(3, o, 2)
    kvb[seq, whole, :] = acc[:, pl.ds(512, 256)].astype(BF16)

    rings, across, across_in = [], [], []
    for k in range(3):
        at = [seq_of(rows[k], column_, core) for column_ in (x, xl, xr, xo)]
        rings.append(RingGather(kvb.at[at[0]], kvb, at, 128, ROWS_KV, sems, 6 * k, right, left))
        there = [seq_of(rows[k], column_, 1 - core) for column_ in (x, xl, xr, xo)]
        across.append(
            [remote(kvb.at[at[n]], kvb.at[at[n]], sems, 18 + 4 * k + n, partner) for n in range(4)]
        )
        across_in.append(
            [remote(kvb.at[at[n]], kvb.at[there[n]], sems, 18 + 4 * k + n, partner) for n in range(4)]
        )
    b1, b2 = seq_of(rows[1], x, core), seq_of(rows[2], x, core)
    up_own = remote(kvb.at[seq], kvb.at[seq], sems, 30, up)
    in_own = remote(kvb.at[seq], kvb.at[b1], sems, 30, up)
    up_next = remote(kvb.at[b1], kvb.at[b1], sems, 31, up)
    in_next = remote(kvb.at[b1], kvb.at[b2], sems, 31, up)
    up_own.start()
    rings[0].start()
    across[0][0].start()
    column(3, o, 0)
    column(3, o, 1)
    for h in range(4):
        piece = acc[:, pl.ds(h * HEAD, HEAD)].astype(BF16)
        qs[heads[h], :] = piece
        qt[pl.ds(0, HEAD), heads[h]] = piece.astype(F32).T.astype(BF16)
    number = lax.broadcasted_iota(jnp.int32, (HEAD, TOK), 0).astype(F32)
    other = jnp.where(number == docs, 0.0, MASKED).astype(BF16)
    for h in range(4):
        qt[pl.ds(HEAD, HEAD), heads[h]] = other
    m_buf[...] = jnp.full(m_buf.shape, MASKED, F32)
    m_run[...] = jnp.full(m_run.shape, MASKED, F32)
    l_buf[...] = jnp.zeros(l_buf.shape, F32)
    o_acc[...] = jnp.zeros(o_acc.shape, F32)
    dq_acc[...] = jnp.zeros(dq_acc.shape, F32)

    def score(b, diagonal):
        key_docs = kvb[b, pl.ds(TOK, 16), :].astype(F32)[0:1, :]
        same = jnp.where(number == key_docs, 1.0, 0.0)
        ka[:, pl.ds(0, HEAD)] = kvb[b, whole, pl.ds(0, HEAD)]
        ka[:, pl.ds(HEAD, HEAD)] = same.T.astype(BF16)
        for h in range(4):
            s = jnp.dot(ka[...], qt[:, heads[h]], preferred_element_type=F32)
            if diagonal:
                key_at = lax.broadcasted_iota(jnp.int32, (TOK, TOK), 0)
                query_at = lax.broadcasted_iota(jnp.int32, (TOK, TOK), 1)
                s = jnp.where(key_at <= query_at, s, MASKED)
            s_buf[seq - b, :, heads[h]] = s
            m_buf[:, heads[h]] = jnp.maximum(m_buf[:, heads[h]], s.reshape(TOK // 8, 8, TOK).max(axis=0))

    def raise_top():
        top = jnp.maximum(jnp.max(m_buf[...], axis=0, keepdims=True), m_run[0:1, :])
        factor = jnp.exp2((m_run[0:1, :] - top) * (SCALE * LOG2E))
        m_run[...] = jnp.broadcast_to(top, m_run.shape)
        l_buf[...] = l_buf[...] * factor
        o_acc[...] = o_acc[...] * factor

    def mix(b):
        values = kvb[b, whole, pl.ds(HEAD, HEAD)]
        for h in range(4):
            s = s_buf[seq - b, :, heads[h]]
            p = jnp.exp2((s - m_run[0:1, heads[h]]) * (SCALE * LOG2E))
            l_buf[:, heads[h]] += p.reshape(TOK // 8, 8, TOK).sum(axis=0)
            o_acc[:, heads[h]] += lax.dot_general(
                values, p.astype(BF16), TN, preferred_element_type=F32
            )

    def sweep(step, lo, hi):
        def one(b, carry):
            step(b)
            return carry

        lax.fori_loop(lo, hi, one, 0)

    low1 = jnp.maximum(8 * y - 8, 0)
    low2 = jnp.maximum(seq - (BAND - 1), 0)
    score(seq, True)
    rings[0].forward()
    in_own.wait_recv()
    up_next.start()
    rings[1].start()
    across[1][0].start()
    rings[0].wait_left()
    across[0][1].start()
    rings[0].wait_right()
    across[0][2].start()
    in_next.wait_recv()
    rings[2].start()
    across[2][0].start()
    rings[0].wait_far()
    across[0][3].start()
    g_ring.forward()
    rings[1].forward()
    for copy in across_in[0]:
        copy.wait_recv()
    sweep(lambda b: score(b, False), 8 * y, seq)
    raise_top()
    rings[1].wait_left()
    across[1][1].start()
    rings[1].wait_right()
    across[1][2].start()
    rings[1].wait_far()
    across[1][3].start()
    rings[2].forward()
    sweep(mix, 8 * y, seq + 1)
    for copy in across_in[1]:
        copy.wait_recv()
    sweep(lambda b: score(b, False), low1, 8 * y)
    raise_top()
    rings[2].wait_left()
    across[2][1].start()
    rings[2].wait_right()
    across[2][2].start()
    rings[2].wait_far()
    across[2][3].start()
    sweep(mix, low1, 8 * y)
    g_ring.wait_left()
    fold_grad(1, l)
    for copy in across_in[2]:
        copy.wait_recv()
    sweep(lambda b: score(b, False), low2, low1)
    raise_top()
    sweep(mix, low2, low1)

    inverse = 1.0 / jnp.sum(l_buf[...], axis=0, keepdims=True)
    li_buf[...] = jnp.broadcast_to(inverse, (8, 1024))
    for h in range(4):
        mixed = o_acc[:, heads[h]] * inverse[:, h * TOK : (h + 1) * TOK]
        att[:, pl.ds(h * HEAD, HEAD)] = mixed.T.astype(BF16)
    g_ring.wait_right()
    fold_grad(2, r)
    g_ring.wait_far()
    fold_grad(3, o)
    g_ring.finish()
    for h in range(4):
        grad = go_acc[:, pl.ds(h * HEAD, HEAD)].astype(BF16)
        do_buf[heads[h], :] = grad
        grad = grad.astype(F32)
        dot_buf[:, heads[h]] = grad.T.astype(BF16)
        mixed = att[:, pl.ds(h * HEAD, HEAD)].astype(F32)
        d_buf[:, heads[h]] = jnp.broadcast_to(
            jnp.sum((grad * mixed).T, axis=0, keepdims=True), (8, TOK)
        )

    def branch_term(slot):
        g_buf[slot] = jnp.dot(att[...], w_out[slot], preferred_element_type=F32).astype(BF16)

    b_ring = RingReduce(
        lambda slot, part: g_buf.at[slot, part], brelay, bfinal, slots, HALF, TOK, zsems, 15, zright, zleft
    )
    branch_term(o)
    b_ring.start_far()
    branch_term(r)
    branch_term(l)
    b_ring.start_near()

    def back(b, k):
        keys = kvb[b, whole, pl.ds(0, HEAD)]
        values = kvb[b, whole, pl.ds(HEAD, HEAD)]
        key_grad = jnp.zeros((TOK, HEAD), F32)
        value_grad = jnp.zeros((TOK, HEAD), F32)
        for h in range(4):
            s = s_buf[seq - b, :, heads[h]]
            p = jnp.exp2((s - m_run[0:1, heads[h]]) * (SCALE * LOG2E)) * li_buf[0:1, heads[h]]
            dp = jnp.dot(values, dot_buf[:, heads[h]], preferred_element_type=F32)
            ds = (p * (dp - d_buf[0:1, heads[h]])).astype(BF16)
            value_grad += jnp.dot(p.astype(BF16), do_buf[heads[h], :], preferred_element_type=F32)
            key_grad += jnp.dot(ds, qs[heads[h], :], preferred_element_type=F32)
            dq_acc[:, heads[h]] += lax.dot_general(keys, ds, TN, preferred_element_type=F32)
        i = b - 8 * (y - k)
        to = dkv.at[k, lax.div(i, 2), lax.rem(i, 2)]
        to[:, pl.ds(0, HEAD)] = (key_grad * SCALE).astype(BF16)
        to[:, pl.ds(HEAD, HEAD)] = value_grad.astype(BF16)

    over = [remote(dkv.at[k, :, 1 - core], twin.at[k], sems, 32 + k, partner) for k in range(3)]
    sum_rings = [
        RingReduce(
            lambda slot, part, k=k: sums.at[k, slot, part],
            xrelay.at[k], xfinal.at[k], (x, xl, xr, xo), HALF, TOK, sems, 35 + 6 * k, right, left,
        )
        for k in range(3)
    ]

    def open_ring(k):
        over[k].wait_recv()

        def add(i, carry):
            sums[k, i] = (dkv[k, i, core].astype(F32) + twin[k, i].astype(F32)).astype(BF16)
            return carry

        lax.fori_loop(0, 4, add, 0)
        sum_rings[k].start_far()
        sum_rings[k].start_near()

    far_up = remote(yown.at[0], ynear.at[0], sems, 53, down)
    near_up = remote(yown.at[1], ynear.at[1], sems, 54, down)
    mid1 = jnp.maximum(8 * y - 4, 0)
    mid0 = jnp.minimum(8 * y + 4, seq)
    sweep(lambda b: back(b, 2), low2, low1)
    over[2].start()
    sweep(lambda b: back(b, 1), low1, mid1)
    open_ring(2)
    b_ring.forward()
    sweep(lambda b: back(b, 1), mid1, 8 * y)
    over[1].start()
    sum_rings[2].forward()
    sweep(lambda b: back(b, 0), 8 * y, mid0)
    open_ring(1)
    yown[0] = sum_rings[2].wait_total()(whole).astype(BF16)
    far_up.start()
    sweep(lambda b: back(b, 0), mid0, seq + 1)
    over[0].start()
    sum_rings[1].forward()
    branch_term(me)
    grads_q = dq_acc[...] * SCALE
    for h in range(4):
        grads[:, pl.ds(h * HEAD, HEAD)] = grads_q[:, h * TOK : (h + 1) * TOK].T.astype(BF16)
    open_ring(0)
    total = sum_rings[1].wait_total()(whole)
    far_up.wait_recv()
    yown[1] = (total + ynear[0].astype(F32)).astype(BF16)
    near_up.start()
    sum_rings[0].forward()
    dots = jnp.zeros((TOK, 1), F32)
    for h in range(4):
        dots += jnp.sum(
            qs[heads[h], :].astype(F32) * grads[:, pl.ds(h * HEAD, HEAD)].astype(F32), axis=-1, keepdims=True
        )
    total = b_ring.wait_total()
    for part in (pl.ds(0, HALF), pl.ds(HALF, HALF)):
        branch_ref[part, :] = total(part)
    total = sum_rings[0].wait_total()(whole)
    near_up.wait_recv()
    grads[:, pl.ds(512, 256)] = (total + ynear[1].astype(F32)).astype(BF16)

    def norm_term(slot):
        for i in range(4):
            at = pl.ds(pl.multiple_of(slot * COLS + i * 256, 256), 256)
            piece = lax.dot_general(grads[...], weights[at, :], NT, preferred_element_type=F32)
            x_buf[slot, :, pl.ds(i * 256, 256)] = piece.astype(BF16)

    x_ring.finish()
    n_ring = RingReduce(
        lambda slot, part: x_buf.at[slot, part], nrelay, nfinal, slots, HALF, TOK, zsems, 21, zright, zleft
    )
    norm_term(o)
    n_ring.start_far()
    norm_term(r)
    norm_term(l)
    n_ring.start_near()
    dots += jnp.sum(
        kvb[seq, whole, :].astype(F32) * grads[:, pl.ds(512, 256)].astype(F32), axis=-1, keepdims=True
    )
    mine[1] = jnp.broadcast_to(dots, (TOK, 128)).T[0:8, :]
    small_dots = exchange(1, 27)
    for copy in small_dots:
        copy.start()
    norm_term(me)
    n_ring.forward()
    for copy in small_dots:
        copy.wait_recv()
    dot_ref[...] = mine[1] + theirs[1, 0] + theirs[1, 1] + theirs[1, 2]
    total = n_ring.wait_total()
    for part in (pl.ds(0, HALF), pl.ds(HALF, HALF)):
        out_ref[part, :] = total(part)
    for copy in small + small_dots + over + [far_up, near_up, up_own, up_next]:
        copy.wait_send()
    for ring in rings + sum_rings + [b_ring, n_ring]:
        ring.finish()
    for k in range(3):
        for n in range(4):
            across[k][n].wait_send()


def block(x, g, docs, gain, w_query, w_key, w_value, w_out):
    return pl.pallas_call(
        block_kernel,
        name="block",
        out_shape=(
            jax.ShapeDtypeStruct((TOK, COLS), F32),
            jax.ShapeDtypeStruct((TOK, COLS), F32),
            jax.ShapeDtypeStruct((8, TOK), F32),
            jax.ShapeDtypeStruct((TOK, 128), F32),
        ),
        in_specs=[ANY, ANY, VM, VM, ANY, ANY, ANY, ANY],
        out_specs=(VM, VM, VM, VM),
        scratch_shapes=[
            pltpu.VMEM((4, TOK, COLS), BF16),
            pltpu.VMEM((4, TOK, COLS), BF16),
            pltpu.VMEM((WIDTH, 768), BF16),
            pltpu.VMEM((4, 512, COLS), BF16),
            pltpu.VMEM((TOK, 768), F32),
            pltpu.VMEM((TOK, 512), F32),
            pltpu.VMEM((TOK, COLS), BF16),
            pltpu.VMEM((2, 8, TOK), F32),
            pltpu.VMEM((2, 3, 8, TOK), F32),
            pltpu.VMEM((32, ROWS_KV, 256), BF16),
            pltpu.VMEM((BAND, TOK, 1024), F32),
            pltpu.VMEM((TOK, 256), BF16),
            pltpu.VMEM((256, 1024), BF16),
            pltpu.VMEM((1024, HEAD), BF16),
            pltpu.VMEM((HEAD, 1024), BF16),
            pltpu.VMEM((1024, HEAD), BF16),
            pltpu.VMEM((HEAD, 1024), F32),
            pltpu.VMEM((HEAD, 1024), F32),
            pltpu.VMEM((8, 1024), F32),
            pltpu.VMEM((8, 1024), F32),
            pltpu.VMEM((8, 1024), F32),
            pltpu.VMEM((8, 1024), F32),
            pltpu.VMEM((8, 1024), F32),
            pltpu.VMEM((TOK, 512), BF16),
            pltpu.VMEM((3, 4, 2, TOK, 256), BF16),
            pltpu.VMEM((3, 4, TOK, 256), BF16),
            pltpu.VMEM((3, 4, TOK, 256), BF16),
            pltpu.VMEM((3, 2, HALF, 256), BF16),
            pltpu.VMEM((3, 2, TOK, 256), BF16),
            pltpu.VMEM((2, TOK, 256), BF16),
            pltpu.VMEM((2, TOK, 256), BF16),
            pltpu.VMEM((2, HALF, COLS), BF16),
            pltpu.VMEM((2, TOK, COLS), BF16),
            pltpu.VMEM((2, HALF, COLS), BF16),
            pltpu.VMEM((2, TOK, COLS), BF16),
            pltpu.VMEM((TOK, 768), BF16),
            DMA((18,)),
            DMA((30,)),
            DMA((30,)),
            DMA((55,)),
            DMA((55,)),
        ],
        compiler_params=pltpu.CompilerParams(
            collective_id=0, has_side_effects=True, vmem_limit_bytes=63 * MIB
        ),
    )(x, g, docs, gain, w_query, w_key, w_value, w_out)


def per_device(
    y_first, x_second, grad_first, grad_second, doc_ids, norm_gain, w_query, w_key, w_value, w_out
):
    mp = lax.axis_index("mp")
    branch, shared, dots, inverse = block(
        x_second, grad_first, doc_ids.reshape(1, TOK), norm_gain.reshape(1, WIDTH),
        w_query, w_key, w_value, w_out,
    )
    x_first = y_first.astype(F32) - branch
    inverse = inverse[:, :1]
    unit = x_second.astype(F32) * inverse
    gain = lax.dynamic_slice_in_dim(norm_gain, mp * COLS, COLS, 0)
    mean = (dots[0] * (1.0 / WIDTH))[:, None]
    x_grad = grad_second.astype(F32) + inverse * (shared * gain - unit * mean)
    return (x_first, x_grad)


def solution(mesh):
    placed = (
        P("seq", "mp"),
        P("seq", "mp"),
        P("seq", "mp"),
        P("seq", "mp"),
        P("seq"),
        P(),
        P(None, "mp"),
        P(None, "mp"),
        P(None, "mp"),
        P("mp", None),
    )
    return jax.shard_map(
        per_device,
        mesh=mesh,
        in_specs=placed,
        out_specs=(P("seq", "mp"), P("seq", "mp")),
        check_vma=False,
    )
```

```python
import jax
import jax.numpy as jnp
from jax import lax
from jax.experimental import pallas as pl
from jax.experimental.pallas import tpu as pltpu
from jax.sharding import PartitionSpec as P

HEAD = 128
EPSILON = 1e-05
MASKED = -1e30
SCALE = HEAD**-0.5
LOG2E = 1.4426950408889634
TOK = 256
HALF = TOK // 2
COLS = 1024
WIDTH = 4096
BAND = 17
ROWS_KV = TOK + 16
MIB = 1 << 20
NT = (((1,), (1,)), ((), ()))
TN = (((0,), (0,)), ((), ()))
F32 = jnp.float32
BF16 = jnp.bfloat16


def place():
    seq, mp = lax.axis_index("seq"), lax.axis_index("mp")
    core = lax.rem(seq, 2)
    x = lax.rem(lax.div(seq, 2), 4)
    y = lax.div(seq, 8)
    return seq, mp, y, x, core


def seq_of(y, x, core):
    return y * 8 + x * 2 + core


def plus(a, b, n=4):
    return lax.rem(a + (b + n) % n, n)


def remote(src, dst, sems, index, device):
    send, recv = sems
    return pltpu.make_async_remote_copy(
        src_ref=src,
        dst_ref=dst,
        send_sem=send.at[index],
        recv_sem=recv.at[index],
        device_id=device,
        device_id_type=pl.DeviceIdType.MESH,
    )


def greet(devices):
    barrier = pltpu.get_barrier_semaphore()
    for device in devices:
        pl.semaphore_signal(barrier, inc=1, device_id=device, device_id_type=pl.DeviceIdType.MESH)
    return lambda: pl.semaphore_wait(barrier, len(devices))


class RingGather:
    def __init__(self, own, buf, slots, first, half, rows, sems, base, right, left, at=None):
        me, l, r, o = slots
        a, b = pl.ds(first, half), pl.ds(first + half, rows - half)
        at = at or (lambda slot, part: buf.at[slot, part])
        take = (lambda part: own.at[part]) if own is not None else (lambda part: at(me, part))
        mk = lambda src, dst, i, dev: remote(src, dst, sems, base + i, dev)
        self.out = [
            mk(take(a), at(me, a), 0, right),
            mk(take(b), at(me, b), 1, right),
            mk(take(b), at(me, b), 2, left),
            mk(take(a), at(me, a), 3, left),
            mk(at(l, a), at(l, a), 4, right),
            mk(at(r, b), at(r, b), 5, left),
        ]
        self.inn = [
            mk(take(a), at(l, a), 0, right),
            mk(take(b), at(l, b), 1, right),
            mk(take(b), at(r, b), 2, left),
            mk(take(a), at(r, a), 3, left),
            mk(take(a), at(o, a), 4, right),
            mk(take(b), at(o, b), 5, left),
        ]

    def start_first(self):
        self.out[0].start()
        self.out[2].start()

    def start_second(self):
        self.out[1].start()
        self.out[3].start()

    def start(self):
        self.start_first()
        self.start_second()

    def forward(self):
        self.inn[0].wait_recv()
        self.out[4].start()
        self.inn[2].wait_recv()
        self.out[5].start()

    def wait_left(self):
        self.inn[1].wait_recv()

    def wait_right(self):
        self.inn[3].wait_recv()

    def wait_far(self):
        self.inn[4].wait_recv()
        self.inn[5].wait_recv()

    def finish(self):
        for copy in self.out:
            copy.wait_send()


class RingReduce:
    def __init__(self, parts, relay, finals, slots, half, rows, sems, base, right, left):
        me, l, r, o = slots
        a, b = pl.ds(0, half), pl.ds(half, rows - half)
        self.parts, self.relay, self.finals = parts, relay, finals
        self.slots, self.a, self.b = slots, a, b
        mk = lambda src, dst, i, dev: remote(src, dst, sems, base + i, dev)
        self.out = [
            mk(parts(o, a), relay.at[0], 0, right),
            mk(parts(o, b), relay.at[1], 1, left),
            mk(parts(r, b), finals.at[0, b], 2, right),
            mk(parts(l, a), finals.at[1, a], 3, left),
            mk(parts(r, a), finals.at[0, a], 4, right),
            mk(parts(l, b), finals.at[1, b], 5, left),
        ]

    def start_far(self):
        self.out[0].start()
        self.out[1].start()

    def start_near(self):
        self.out[2].start()
        self.out[3].start()

    def forward(self):
        me, l, r, o = self.slots
        for i, slot, part in ((0, r, self.a), (1, l, self.b)):
            self.out[i].wait_recv()
            piece = self.parts(slot, part)
            piece[...] = (piece[...].astype(F32) + self.relay[i].astype(F32)).astype(BF16)
            self.out[4 + i].start()

    def wait_total(self):
        for i in (2, 3, 4, 5):
            self.out[i].wait_recv()
        me = self.slots[0]
        return lambda part: (
            self.parts(me, part)[...].astype(F32)
            + self.finals[0, part].astype(F32)
            + self.finals[1, part].astype(F32)
        )

    def finish(self):
        for copy in self.out:
            copy.wait_send()


def z_places(seq, mp):
    right, left, far = plus(mp, 1), plus(mp, -1), plus(mp, 2)
    return (mp, left, right, far), (seq, right), (seq, left), (seq, far)


VM = pl.BlockSpec(memory_space=pltpu.VMEM)
ANY = pl.BlockSpec(memory_space=pl.ANY)
DMA = pltpu.SemaphoreType.DMA


def block_kernel(x_ref, g_ref, y_ref, g2_ref, docs_ref, gain_ref, wq_ref, wk_ref, wv_ref, wo_ref,
                 first_ref, grad_ref, inv_ref, x_own, y_own, g2_own, p_buf, ds_buf, wkv, kv_all,
                 x_buf, g_buf, weights, w_out, acc, go_acc, scaled, mine, theirs, kvb, s_buf, ka, qt, qs,
                 dot_buf, o_acc, dq_acc, m_buf, m_run, t_buf, l_buf, d_buf, att, dkv, twin, sums,
                 xrelay, xfinal, ynear, yown, brelay, bfinal, nrelay, nfinal, grads,
                 lsem, zsend, zrecv, send, recv):
    seq, mp, y, x, core = place()
    slots, zright, zleft, zfar = z_places(seq, mp)
    me, l, r, o = slots
    zsems, sems = (zsend, zrecv), (send, recv)
    xr, xl, xo = plus(x, 1), plus(x, -1), plus(x, 2)
    up, down = (seq_of(plus(y, 1), x, core), mp), (seq_of(plus(y, -1), x, core), mp)
    right, left = (seq_of(y, xr, core), mp), (seq_of(y, xl, core), mp)
    partner = (seq_of(y, x, 1 - core), mp)
    above = (seq_of(plus(y, 2), x, core), mp)
    yu, yd, yo = plus(y, 1), plus(y, -1), plus(y, 2)
    rows = [plus(y, -k) for k in range(3)]
    heads = [pl.ds(h * TOK, TOK) for h in range(4)]
    whole = pl.ds(0, TOK)

    met = greet([up, down, above, right, left, partner, zright, zleft, zfar])

    x_load = pltpu.make_async_copy(x_ref, x_buf.at[me], lsem.at[0])
    x_load.start()
    loads = []
    for n, slot in enumerate((me, l, r, o)):
        at = pl.ds(pl.multiple_of(slot * COLS, COLS), COLS)
        group = []
        for i, (w, lo, hi) in enumerate(((wq_ref, 0, 512), (wk_ref, 512, 640), (wv_ref, 640, 768))):
            copy = pltpu.make_async_copy(w.at[at], weights.at[at, pl.ds(lo, hi - lo)], lsem.at[1 + 3 * n + i])
            copy.start()
            group.append(copy)
        loads.append(group)
    g_load = pltpu.make_async_copy(g_ref, g_buf.at[me], lsem.at[13])
    g_load.start()
    w_loads = []
    for n, slot in enumerate((me, l, r, o)):
        cols = pl.ds(pl.multiple_of(slot * COLS, COLS), COLS)
        copy = pltpu.make_async_copy(wo_ref.at[:, cols], w_out.at[slot], lsem.at[14 + n])
        copy.start()
        w_loads.append(copy)
    late = []
    for i, (src, dst) in enumerate(((x_ref, x_own), (y_ref, y_own), (g2_ref, g2_own))):
        copy = pltpu.make_async_copy(src, dst, lsem.at[18 + i])
        copy.start()
        late.append(copy)

    x_rings = [
        RingGather(x_ref, x_buf, slots, i * HALF, HALF // 2, HALF, zsems, 30 * i, zright, zleft) for i in range(2)
    ]
    met()
    x_rings[0].start_first()
    x_load.wait()
    values = x_buf[me].astype(F32)
    squares = jnp.sum(values * values, axis=-1, keepdims=True)
    mine[0] = jnp.broadcast_to(squares, (TOK, 128)).T[0:8, :]

    def exchange(which, base):
        return [
            remote(mine.at[which], theirs.at[which, i], zsems, base + i, device)
            for i, device in enumerate((zright, zleft, zfar))
        ]

    small = exchange(0, 6)
    for copy in small:
        copy.start()
    x_rings[0].start_second()
    docs = docs_ref[...].astype(F32)
    kvb[seq, pl.ds(TOK, 16), :] = jnp.broadcast_to(docs, (16, TOK)).astype(BF16)

    def clear(i, carry):
        for k in range(3):
            for c in range(2):
                dkv[k, i, c] = jnp.zeros((TOK, 256), BF16)
        return carry

    lax.fori_loop(0, 4, clear, 0)
    for copy in small:
        copy.wait_recv()
    squares = mine[0] + theirs[0, 0] + theirs[0, 1] + theirs[0, 2]
    inverse = lax.rsqrt(squares[0:1, :] * (1.0 / WIDTH) + EPSILON)
    inv_ref[...] = jnp.broadcast_to(inverse, (128, TOK)).T

    def column(n, slot, i, part):
        at = pl.ds(pl.multiple_of(slot * COLS, COLS), COLS)
        cols = pl.ds(i * 256, 256)
        term = jnp.dot(scaled[part, :], weights[at, cols], preferred_element_type=F32)
        acc[part, cols] = term if n == 0 else acc[part, cols] + term

    def scale_rows(slot, part):
        gain = gain_ref[:, pl.ds(pl.multiple_of(slot * COLS, COLS), COLS)]
        scaled[part, :] = (x_buf[slot, part, :].astype(F32) * inv_ref[part, 0:1] * gain).astype(BF16)

    def fold(n, slot, part):
        scale_rows(slot, part)
        for i in range(3):
            column(n, slot, i, part)

    def fold_grad(n, slot):
        w_loads[n].wait()
        term = lax.dot_general(g_buf[slot], w_out[slot], NT, preferred_element_type=F32)
        go_acc[...] = term if n == 0 else go_acc[...] + term

    halves = (pl.ds(0, HALF), pl.ds(HALF, HALF))
    sent = (pl.ds(0, HALF), pl.ds(HALF, ROWS_KV - HALF))
    rings, across, across_in = [], [], []
    for k in range(3):
        at = [seq_of(rows[k], column_, core) for column_ in (x, xl, xr, xo)]
        there = [seq_of(rows[k], column_, 1 - core) for column_ in (x, xl, xr, xo)]
        rings.append([
            RingGather(
                kvb.at[at[0]], kvb, at, i * HALF, 64, (HALF, ROWS_KV - HALF)[i], sems, 12 * k + 6 * i, right, left
            )
            for i in range(2)
        ])
        across.append([
            [remote(kvb.at[at[n], sent[i]], kvb.at[at[n], sent[i]], sems, 36 + 8 * k + 2 * n + i, partner)
             for n in range(4)] for i in range(2)
        ])
        across_in.append([
            [remote(kvb.at[at[n], sent[i]], kvb.at[there[n], sent[i]], sems, 36 + 8 * k + 2 * n + i, partner)
             for n in range(4)] for i in range(2)
        ])
    b1, b2 = seq_of(rows[1], x, core), seq_of(rows[2], x, core)

    def lift(dst, base, device):
        return [remote(kvb.at[seq, sent[i]], kvb.at[dst, sent[i]], sems, base + i, device) for i in range(2)]

    up_own, in_own = lift(seq, 60, up), lift(b1, 60, up)
    up_next, in_next = lift(seq, 62, above), lift(b2, 62, above)

    def launch(i):
        kvb[seq, halves[i], :] = acc[halves[i], pl.ds(512, 256)].astype(BF16)
        up_own[i].start()
        up_next[i].start()
        rings[0][i].start()
        across[0][i][0].start()

    def second_row(i):
        in_own[i].wait_recv()
        rings[1][i].start()
        across[1][i][0].start()

    def third_row(i):
        in_next[i].wait_recv()
        rings[2][i].start()
        across[2][i][0].start()

    def near(k, i):
        rings[k][i].wait_left()
        across[k][i][1].start()
        rings[k][i].wait_right()
        across[k][i][2].start()

    def pass_on(k, i):
        near(k, i)
        rings[k][i].wait_far()
        across[k][i][3].start()

    g_ring = RingGather(g_ref, g_buf, slots, 0, HALF, TOK, zsems, 9, zright, zleft)
    for group in loads:
        for copy in group:
            copy.wait()
    slot = 2 * x + core
    pieces = []
    for i, (target, device) in enumerate(((r, zright), (l, zleft), (o, zfar))):
        at = pl.ds(pl.multiple_of(target * COLS + seq * 32, 32), 32)
        pieces.append(remote(weights.at[at, pl.ds(512, 256)], wkv.at[i, y, slot], zsems, 36 + i, device))
    y_pieces = RingGather(
        None, None, (y, yd, yu, yo), 0, 16, 32, sems, 87, up, down,
        at=lambda row, part: wkv.at[:, row, slot, part],
    )
    x_pieces = RingGather(
        None, None, (x, xl, xr, xo), 0, 16, 32, sems, 93, right, left,
        at=lambda column_, part: wkv.at[:, :, 2 * column_ + core, part],
    )
    over_pieces = [
        remote(wkv.at[:, :, 2 * n + core], wkv.at[:, :, 2 * n + core], sems, 99 + n, partner) for n in range(4)
    ]
    over_in = [
        remote(wkv.at[:, :, 2 * n + core], wkv.at[:, :, 2 * n + 1 - core], sems, 99 + n, partner) for n in range(4)
    ]
    x_rings[0].forward()
    for copy in pieces:
        copy.start()
    x_rings[1].start()
    fold(0, me, whole)
    x_rings[0].wait_left()
    fold(1, l, halves[0])
    x_rings[0].wait_right()
    fold(2, r, halves[0])
    x_rings[0].wait_far()
    scale_rows(o, halves[0])
    column(3, o, 2, halves[0])
    launch(0)
    x_rings[1].forward()
    g_ring.start()
    column(3, o, 0, halves[0])
    column(3, o, 1, halves[0])
    rings[0][0].forward()
    second_row(0)
    third_row(0)
    x_rings[1].wait_left()
    fold(1, l, halves[1])
    x_rings[1].wait_right()
    fold(2, r, halves[1])
    pass_on(0, 0)
    rings[1][0].forward()
    x_rings[1].wait_far()
    scale_rows(o, halves[1])
    column(3, o, 2, halves[1])
    launch(1)
    for copy in pieces:
        copy.wait_recv()
    y_pieces.start()
    rings[2][0].forward()
    column(3, o, 0, halves[1])
    column(3, o, 1, halves[1])
    pass_on(1, 0)
    for h in range(4):
        piece = acc[:, pl.ds(h * HEAD, HEAD)].astype(BF16)
        qs[heads[h], :] = piece
        qt[pl.ds(0, HEAD), heads[h]] = piece.astype(F32).T.astype(BF16)
    number = lax.broadcasted_iota(jnp.int32, (HEAD, TOK), 0).astype(F32)
    other = jnp.where(number == docs, 0.0, MASKED).astype(BF16)
    for h in range(4):
        qt[pl.ds(HEAD, HEAD), heads[h]] = other
    m_buf[...] = jnp.full(m_buf.shape, MASKED, F32)
    m_run[...] = jnp.full(m_run.shape, MASKED, F32)
    l_buf[...] = jnp.zeros(l_buf.shape, F32)
    o_acc[...] = jnp.zeros(o_acc.shape, F32)
    dq_acc[...] = jnp.zeros(dq_acc.shape, F32)

    def score(b, diagonal):
        key_docs = kvb[b, pl.ds(TOK, 16), :].astype(F32)[0:1, :]
        same = jnp.where(number == key_docs, 1.0, 0.0)
        ka[:, pl.ds(0, HEAD)] = kvb[b, whole, pl.ds(0, HEAD)]
        ka[:, pl.ds(HEAD, HEAD)] = same.T.astype(BF16)
        for h in range(4):
            s = jnp.dot(ka[...], qt[:, heads[h]], preferred_element_type=F32)
            if diagonal:
                key_at = lax.broadcasted_iota(jnp.int32, (TOK, TOK), 0)
                query_at = lax.broadcasted_iota(jnp.int32, (TOK, TOK), 1)
                s = jnp.where(key_at <= query_at, s, MASKED)
            s_buf[seq - b, :, heads[h]] = s
            m_buf[:, heads[h]] = jnp.maximum(m_buf[:, heads[h]], s.reshape(TOK // 8, 8, TOK).max(axis=0))

    def raise_top():
        top = jnp.maximum(jnp.max(m_buf[...], axis=0, keepdims=True), m_run[0:1, :])
        factor = jnp.exp2((m_run[0:1, :] - top) * (SCALE * LOG2E))
        m_run[...] = jnp.broadcast_to(top, m_run.shape)
        t_buf[...] = m_run[...] * (SCALE * LOG2E)
        l_buf[...] = l_buf[...] * factor
        o_acc[...] = o_acc[...] * factor

    def mix(b):
        values = kvb[b, whole, pl.ds(HEAD, HEAD)]
        for h in range(4):
            s = s_buf[seq - b, :, heads[h]]
            p = jnp.exp2(s * (SCALE * LOG2E) - t_buf[0:1, heads[h]])
            l_buf[:, heads[h]] += p.reshape(TOK // 8, 8, TOK).sum(axis=0)
            o_acc[:, heads[h]] += lax.dot_general(
                values, p.astype(BF16), TN, preferred_element_type=F32
            )

    def sweep(step, lo, hi):
        def one(b, carry):
            step(b)
            return carry

        lax.fori_loop(lo, hi, one, 0)

    def fold_grad_own():
        g_load.wait()
        fold_grad(0, me)

    low1 = jnp.maximum(8 * y - 8, 0)
    mid1 = jnp.maximum(8 * y - 4, 0)
    mid0 = jnp.minimum(8 * y + 4, seq)
    low2 = jnp.maximum(seq - (BAND - 1), 0)
    rings[0][1].forward()
    second_row(1)
    third_row(1)
    score(seq, True)
    pass_on(2, 0)
    pass_on(0, 1)
    y_pieces.forward()
    rings[1][1].forward()
    rings[2][1].forward()
    for copies in across_in[0]:
        for copy in copies:
            copy.wait_recv()
    sweep(lambda b: score(b, False), 8 * y, mid0)
    g_ring.forward()
    sweep(lambda b: score(b, False), mid0, seq)
    raise_top()
    pass_on(1, 1)
    sweep(mix, 8 * y, mid0)
    pass_on(2, 1)
    sweep(mix, mid0, seq + 1)
    y_pieces.wait_left()
    y_pieces.wait_right()
    y_pieces.wait_far()
    x_pieces.start()
    fold_grad_own()
    for copies in across_in[1]:
        for copy in copies:
            copy.wait_recv()
    sweep(lambda b: score(b, False), low1, 8 * y)
    raise_top()
    sweep(mix, low1, 8 * y)
    g_ring.wait_left()
    fold_grad(1, l)
    g_ring.wait_right()
    fold_grad(2, r)
    for copies in across_in[2]:
        for copy in copies:
            copy.wait_recv()
    sweep(lambda b: score(b, False), low2, low1)
    raise_top()
    sweep(mix, low2, low1)
    x_pieces.forward()
    g_ring.wait_far()
    fold_grad(3, o)
    for h in range(4):
        grad = go_acc[:, pl.ds(h * HEAD, HEAD)].astype(BF16)
        dot_buf[:, heads[h]] = grad.astype(F32).T.astype(BF16)
    g_ring.finish()

    total = jnp.sum(l_buf[...], axis=0, keepdims=True)
    inverse = 1.0 / total
    t_buf[...] = t_buf[...] + jnp.log2(total)
    for h in range(4):
        mixed = (o_acc[:, heads[h]] * inverse[:, h * TOK : (h + 1) * TOK]).astype(BF16).astype(F32)
        att[:, pl.ds(h * HEAD, HEAD)] = mixed.T.astype(BF16)
        delta = jnp.sum(dot_buf[:, heads[h]].astype(F32) * mixed, axis=0, keepdims=True)
        d_buf[:, heads[h]] = jnp.broadcast_to(delta, (8, TOK))

    def branch_term(slot):
        g_buf[slot] = jnp.dot(att[...], w_out[slot], preferred_element_type=F32).astype(BF16)

    b_ring = RingReduce(
        lambda slot, part: g_buf.at[slot, part], brelay, bfinal, slots, HALF, TOK, zsems, 15, zright, zleft
    )
    branch_term(o)
    b_ring.start_far()

    def back(b, k):
        keys = kvb[b, whole, pl.ds(0, HEAD)]
        values = kvb[b, whole, pl.ds(HEAD, HEAD)]
        for h in range(4):
            s = s_buf[seq - b, :, heads[h]]
            p = jnp.exp2(s * (SCALE * LOG2E) - t_buf[0:1, heads[h]])
            dp = jnp.dot(values, dot_buf[:, heads[h]], preferred_element_type=F32)
            p_buf[:, heads[h]] = p.astype(BF16)
            ds_buf[:, heads[h]] = (p * (dp - d_buf[0:1, heads[h]])).astype(BF16)
        dq_acc[...] += lax.dot_general(keys, ds_buf[...], TN, preferred_element_type=F32)
        value_grad = lax.dot_general(dot_buf[...], p_buf[...], NT, preferred_element_type=F32)
        key_grad = lax.dot_general(qt[pl.ds(0, HEAD), :], ds_buf[...], NT, preferred_element_type=F32)
        i = b - 8 * (y - k)
        to = dkv.at[k, lax.div(i, 2), lax.rem(i, 2)]
        to[pl.ds(0, HEAD), :] = (key_grad * SCALE).astype(BF16)
        to[pl.ds(HEAD, HEAD), :] = value_grad.astype(BF16)

    over = [remote(dkv.at[k, :, 1 - core], twin.at[k], sems, 64 + k, partner) for k in range(3)]
    sum_rings = [
        RingReduce(
            lambda slot, part, k=k: sums.at[k, slot, part],
            xrelay.at[k], xfinal.at[k], (x, xl, xr, xo), HALF, TOK, sems, 67 + 6 * k, right, left,
        )
        for k in range(3)
    ]

    def open_ring(k):
        over[k].wait_recv()

        def add(i, carry):
            sums[k, i] = (dkv[k, i, core].astype(F32) + twin[k, i].astype(F32)).astype(BF16)
            return carry

        lax.fori_loop(0, 4, add, 0)
        sum_rings[k].start_far()
        sum_rings[k].start_near()

    far_up = remote(yown.at[0], ynear.at[0], sems, 85, down)
    near_up = remote(yown.at[1], ynear.at[1], sems, 86, down)
    sweep(lambda b: back(b, 2), low2, low1)
    over[2].start()
    branch_term(r)
    branch_term(l)
    b_ring.start_near()
    sweep(lambda b: back(b, 1), low1, mid1)
    open_ring(2)
    b_ring.forward()
    sweep(lambda b: back(b, 1), mid1, 8 * y)
    over[1].start()
    x_pieces.wait_left()
    x_pieces.wait_right()
    x_pieces.wait_far()
    for copy in over_pieces:
        copy.start()
    sum_rings[2].forward()
    sweep(lambda b: back(b, 0), 8 * y, mid0)
    open_ring(1)
    yown[0] = sum_rings[2].wait_total()(whole).astype(BF16)
    far_up.start()
    sweep(lambda b: back(b, 0), mid0, seq + 1)
    over[0].start()
    grads_q = dq_acc[...] * SCALE
    for h in range(4):
        grads[:, pl.ds(h * HEAD, HEAD)] = grads_q[:, h * TOK : (h + 1) * TOK].T.astype(BF16)
    for ring in x_rings:
        ring.finish()

    def norm_term(slot):
        for i in range(4):
            at = pl.ds(pl.multiple_of(slot * COLS + i * 256, 256), 256)
            piece = lax.dot_general(
                grads[:, pl.ds(0, 512)], weights[at, pl.ds(0, 512)], NT, preferred_element_type=F32
            )
            x_buf[slot, :, pl.ds(i * 256, 256)] = piece.astype(BF16)

    n_ring = RingReduce(
        lambda slot, part: x_buf.at[slot, part], nrelay, nfinal, slots, HALF, TOK, zsems, 21, zright, zleft
    )
    norm_term(o)
    n_ring.start_far()
    sum_rings[1].forward()
    norm_term(r)
    norm_term(l)
    n_ring.start_near()
    open_ring(0)
    total = sum_rings[1].wait_total()(whole)
    far_up.wait_recv()
    yown[1] = (total + ynear[0].astype(F32)).astype(BF16)
    near_up.start()
    sum_rings[0].forward()
    branch_term(me)
    norm_term(me)
    dots = jnp.zeros((TOK, 1), F32)
    for h in range(4):
        dots += jnp.sum(
            qs[heads[h], :].astype(F32) * grads[:, pl.ds(h * HEAD, HEAD)].astype(F32), axis=-1, keepdims=True
        )
    for copy in late:
        copy.wait()
    total = b_ring.wait_total()
    for part in (pl.ds(0, HALF), pl.ds(HALF, HALF)):
        s_buf[0, part, :] = y_own[part, :].astype(F32) - total(part)
    first_out = pltpu.make_async_copy(s_buf.at[0], first_ref, lsem.at[21])
    first_out.start()
    n_ring.forward()
    total = sum_rings[0].wait_total()(whole)
    near_up.wait_recv()
    total = (total + ynear[1].astype(F32)).astype(BF16).astype(F32).T
    kv_all[me] = total.astype(BF16)
    kv_ring = RingGather(None, kv_all, slots, 0, HALF, TOK, zsems, 39, zright, zleft)
    kv_ring.start()
    dots += jnp.sum(kvb[seq, whole, :].astype(F32) * kv_all[me].astype(F32), axis=-1, keepdims=True)
    mine[1] = jnp.broadcast_to(dots, (TOK, 128)).T[0:8, :]
    small_dots = exchange(1, 27)
    for copy in small_dots:
        copy.start()

    for copy in over_in:
        copy.wait_recv()

    def kv_term(n, slot):
        for i in range(4):
            cols = pl.ds(i * 256, 256)
            if n == 0:
                at = pl.ds(pl.multiple_of(me * COLS + i * 256, 256), 256)
                w = weights[at, pl.ds(512, 256)]
            else:
                w = wkv[n - 1, i].reshape(256, 256)
            term = lax.dot_general(kv_all[slot], w, NT, preferred_element_type=F32)
            s_buf[2, :, cols] = term if n == 0 else s_buf[2, :, cols] + term

    kv_term(0, me)
    kv_ring.forward()
    kv_ring.wait_left()
    kv_term(1, l)
    kv_ring.wait_right()
    kv_term(2, r)
    for copy in small_dots:
        copy.wait_recv()
    mean = (mine[1] + theirs[1, 0] + theirs[1, 1] + theirs[1, 2])[0:1, :] * (1.0 / WIDTH)
    mean = jnp.broadcast_to(mean, (128, TOK)).T
    gain = gain_ref[:, pl.ds(pl.multiple_of(me * COLS, COLS), COLS)]
    total = n_ring.wait_total()
    kv_ring.wait_far()
    kv_term(3, o)
    grad_out = []
    for i in range(2):
        lo, hi, part = i * HALF, (i + 1) * HALF, pl.ds(i * HALF, HALF)
        inverse = inv_ref[part, 0:1]
        unit = x_own[part, :].astype(F32) * inverse
        s_buf[1, part, :] = g2_own[part, :].astype(F32) + inverse * (
            (total(part) + s_buf[2, part, :]) * gain - unit * mean[lo:hi, 0:1]
        )
        copy = pltpu.make_async_copy(s_buf.at[1, part], grad_ref.at[part], lsem.at[22 + i])
        copy.start()
        grad_out.append(copy)
    first_out.wait()
    for copy in grad_out:
        copy.wait()
    for copy in small + small_dots + pieces + over_pieces + over + [far_up, near_up] + up_own + up_next:
        copy.wait_send()
    for ring in rings[0] + rings[1] + rings[2] + sum_rings + [b_ring, n_ring, kv_ring, y_pieces, x_pieces]:
        ring.finish()
    for k in range(3):
        for i in range(2):
            for copy in across[k][i]:
                copy.wait_send()


def block(x, g, y, g2, docs, gain, w_query, w_key, w_value, w_out):
    return pl.pallas_call(
        block_kernel,
        name="block",
        out_shape=(
            jax.ShapeDtypeStruct((TOK, COLS), F32),
            jax.ShapeDtypeStruct((TOK, COLS), F32),
        ),
        in_specs=[ANY, ANY, ANY, ANY, VM, VM, ANY, ANY, ANY, ANY],
        out_specs=(ANY, ANY),
        scratch_shapes=[
            pltpu.VMEM((TOK, 128), F32),
            pltpu.VMEM((TOK, COLS), BF16),
            pltpu.VMEM((TOK, COLS), BF16),
            pltpu.VMEM((TOK, COLS), BF16),
            pltpu.VMEM((TOK, 1024), BF16),
            pltpu.VMEM((TOK, 1024), BF16),
            pltpu.VMEM((3, 4, 8, 32, 256), BF16),
            pltpu.VMEM((4, TOK, 256), BF16),
            pltpu.VMEM((4, TOK, COLS), BF16),
            pltpu.VMEM((4, TOK, COLS), BF16),
            pltpu.VMEM((WIDTH, 768), BF16),
            pltpu.VMEM((4, 512, COLS), BF16),
            pltpu.VMEM((TOK, 768), F32),
            pltpu.VMEM((TOK, 512), F32),
            pltpu.VMEM((TOK, COLS), BF16),
            pltpu.VMEM((2, 8, TOK), F32),
            pltpu.VMEM((2, 3, 8, TOK), F32),
            pltpu.VMEM((32, ROWS_KV, 256), BF16),
            pltpu.VMEM((BAND, TOK, 1024), F32),
            pltpu.VMEM((TOK, 256), BF16),
            pltpu.VMEM((256, 1024), BF16),
            pltpu.VMEM((1024, HEAD), BF16),
            pltpu.VMEM((HEAD, 1024), BF16),
            pltpu.VMEM((HEAD, 1024), F32),
            pltpu.VMEM((HEAD, 1024), F32),
            pltpu.VMEM((8, 1024), F32),
            pltpu.VMEM((8, 1024), F32),
            pltpu.VMEM((8, 1024), F32),
            pltpu.VMEM((8, 1024), F32),
            pltpu.VMEM((8, 1024), F32),
            pltpu.VMEM((TOK, 512), BF16),
            pltpu.VMEM((3, 4, 2, TOK, 256), BF16),
            pltpu.VMEM((3, 4, TOK, 256), BF16),
            pltpu.VMEM((3, 4, TOK, 256), BF16),
            pltpu.VMEM((3, 2, HALF, 256), BF16),
            pltpu.VMEM((3, 2, TOK, 256), BF16),
            pltpu.VMEM((2, TOK, 256), BF16),
            pltpu.VMEM((2, TOK, 256), BF16),
            pltpu.VMEM((2, HALF, COLS), BF16),
            pltpu.VMEM((2, TOK, COLS), BF16),
            pltpu.VMEM((2, HALF, COLS), BF16),
            pltpu.VMEM((2, TOK, COLS), BF16),
            pltpu.VMEM((TOK, 512), BF16),
            DMA((24,)),
            DMA((45,)),
            DMA((45,)),
            DMA((103,)),
            DMA((103,)),
        ],
        compiler_params=pltpu.CompilerParams(
            collective_id=0, has_side_effects=True, vmem_limit_bytes=63 * MIB
        ),
    )(x, g, y, g2, docs, gain, w_query, w_key, w_value, w_out)


def hand_on_kernel(a_ref, b_ref, a_out, b_out, a_buf, b_buf, sem):
    moves = []
    for n, (src, buf, dst) in enumerate(((a_ref, a_buf, a_out), (b_ref, b_buf, b_out))):
        for i in range(2):
            part = pl.ds(i * HALF, HALF)
            take = pltpu.make_async_copy(src.at[part], buf.at[part], sem.at[0, n, i])
            give = pltpu.make_async_copy(buf.at[part], dst.at[part], sem.at[1, n, i])
            take.start()
            moves.append((take, give))
    for take, give in moves:
        take.wait()
        give.start()
    for take, give in moves:
        give.wait()


def hand_on(a, b):
    shape = jax.ShapeDtypeStruct((TOK, COLS), F32)
    return pl.pallas_call(
        hand_on_kernel,
        name="hand_on",
        out_shape=(shape, shape),
        in_specs=[ANY, ANY],
        out_specs=(ANY, ANY),
        scratch_shapes=[
            pltpu.VMEM((TOK, COLS), F32),
            pltpu.VMEM((TOK, COLS), F32),
            DMA((2, 2, 2)),
        ],
        compiler_params=pltpu.CompilerParams(vmem_limit_bytes=63 * MIB),
    )(a, b)


def per_device(
    y_first, x_second, grad_first, grad_second, doc_ids, norm_gain, w_query, w_key, w_value, w_out
):
    first, grad = block(
        x_second, grad_first, y_first, grad_second, doc_ids.reshape(1, TOK), norm_gain.reshape(1, WIDTH),
        w_query, w_key, w_value, w_out,
    )
    return hand_on(first, grad)


def solution(mesh):
    placed = (
        P("seq", "mp"),
        P("seq", "mp"),
        P("seq", "mp"),
        P("seq", "mp"),
        P("seq"),
        P(),
        P(None, "mp"),
        P(None, "mp"),
        P(None, "mp"),
        P("mp", None),
    )
    return jax.shard_map(
        per_device,
        mesh=mesh,
        in_specs=placed,
        out_specs=(P("seq", "mp"), P("seq", "mp")),
        check_vma=False,
    )
```

```python
import jax
import jax.numpy as jnp
from jax import lax
from jax.experimental import pallas as pl
from jax.experimental.pallas import tpu as pltpu
from jax.sharding import PartitionSpec as P

HEAD = 128
EPSILON = 1e-05
MASKED = -1e30
SCALE = HEAD**-0.5
LOG2E = 1.4426950408889634
TOK = 256
HALF = TOK // 2
COLS = 1024
WIDTH = 4096
BAND = 17
ROWS_KV = TOK + 16
MIB = 1 << 20
NT = (((1,), (1,)), ((), ()))
TN = (((0,), (0,)), ((), ()))
F32 = jnp.float32
BF16 = jnp.bfloat16


def place():
    seq, mp = lax.axis_index("seq"), lax.axis_index("mp")
    core = lax.rem(seq, 2)
    x = lax.rem(lax.div(seq, 2), 4)
    y = lax.div(seq, 8)
    return seq, mp, y, x, core


def seq_of(y, x, core):
    return y * 8 + x * 2 + core


def plus(a, b, n=4):
    return lax.rem(a + (b + n) % n, n)


def remote(src, dst, sems, index, device):
    send, recv = sems
    return pltpu.make_async_remote_copy(
        src_ref=src,
        dst_ref=dst,
        send_sem=send.at[index],
        recv_sem=recv.at[index],
        device_id=device,
        device_id_type=pl.DeviceIdType.MESH,
    )


def greet(devices):
    barrier = pltpu.get_barrier_semaphore()
    for device in devices:
        pl.semaphore_signal(barrier, inc=1, device_id=device, device_id_type=pl.DeviceIdType.MESH)
    return lambda: pl.semaphore_wait(barrier, len(devices))


class RingGather:
    def __init__(self, own, buf, slots, first, half, rows, sems, base, right, left, at=None):
        me, l, r, o = slots
        a, b = pl.ds(first, half), pl.ds(first + half, rows - half)
        at = at or (lambda slot, part: buf.at[slot, part])
        take = (lambda part: own.at[part]) if own is not None else (lambda part: at(me, part))
        mk = lambda src, dst, i, dev: remote(src, dst, sems, base + i, dev)
        self.out = [
            mk(take(a), at(me, a), 0, right),
            mk(take(b), at(me, b), 1, right),
            mk(take(b), at(me, b), 2, left),
            mk(take(a), at(me, a), 3, left),
            mk(at(l, a), at(l, a), 4, right),
            mk(at(r, b), at(r, b), 5, left),
        ]
        self.inn = [
            mk(take(a), at(l, a), 0, right),
            mk(take(b), at(l, b), 1, right),
            mk(take(b), at(r, b), 2, left),
            mk(take(a), at(r, a), 3, left),
            mk(take(a), at(o, a), 4, right),
            mk(take(b), at(o, b), 5, left),
        ]

    def start_first(self):
        self.out[0].start()
        self.out[2].start()

    def start_second(self):
        self.out[1].start()
        self.out[3].start()

    def start(self):
        self.start_first()
        self.start_second()

    def forward(self):
        self.inn[0].wait_recv()
        self.out[4].start()
        self.inn[2].wait_recv()
        self.out[5].start()

    def wait_left(self):
        self.inn[1].wait_recv()

    def wait_right(self):
        self.inn[3].wait_recv()

    def wait_far(self):
        self.inn[4].wait_recv()
        self.inn[5].wait_recv()

    def finish(self):
        for copy in self.out:
            copy.wait_send()


class RingReduce:
    def __init__(self, parts, relay, finals, slots, half, rows, sems, base, right, left):
        me, l, r, o = slots
        a, b = pl.ds(0, half), pl.ds(half, rows - half)
        self.parts, self.relay, self.finals = parts, relay, finals
        self.slots, self.a, self.b = slots, a, b
        mk = lambda src, dst, i, dev: remote(src, dst, sems, base + i, dev)
        self.out = [
            mk(parts(o, a), relay.at[0], 0, right),
            mk(parts(o, b), relay.at[1], 1, left),
            mk(parts(r, b), finals.at[0, b], 2, right),
            mk(parts(l, a), finals.at[1, a], 3, left),
            mk(parts(r, a), finals.at[0, a], 4, right),
            mk(parts(l, b), finals.at[1, b], 5, left),
        ]

    def start_far(self):
        self.out[0].start()
        self.out[1].start()

    def start_near(self):
        self.out[2].start()
        self.out[3].start()

    def forward(self):
        me, l, r, o = self.slots
        for i, slot, part in ((0, r, self.a), (1, l, self.b)):
            self.out[i].wait_recv()
            piece = self.parts(slot, part)
            piece[...] = (piece[...].astype(F32) + self.relay[i].astype(F32)).astype(BF16)
            self.out[4 + i].start()

    def wait_total(self):
        for i in (2, 3, 4, 5):
            self.out[i].wait_recv()
        me = self.slots[0]
        return lambda part: (
            self.parts(me, part)[...].astype(F32)
            + self.finals[0, part].astype(F32)
            + self.finals[1, part].astype(F32)
        )

    def finish(self):
        for copy in self.out:
            copy.wait_send()


def z_places(seq, mp):
    right, left, far = plus(mp, 1), plus(mp, -1), plus(mp, 2)
    return (mp, left, right, far), (seq, right), (seq, left), (seq, far)


VM = pl.BlockSpec(memory_space=pltpu.VMEM)
ANY = pl.BlockSpec(memory_space=pl.ANY)
DMA = pltpu.SemaphoreType.DMA


def block_kernel(x_ref, g_ref, y_ref, g2_ref, docs_ref, gain_ref, wq_ref, wk_ref, wv_ref, wo_ref,
                 first_ref, grad_ref, inv_ref, x_own, y_own, g2_own, p_buf, ds_buf, wkv, kv_all,
                 x_buf, g_buf, weights, w_out, acc, go_acc, scaled, mine, theirs, kvb, s_buf, ka, qt, qs,
                 dot_buf, o_acc, dq_acc, m_buf, m_run, t_buf, l_buf, d_buf, att, dkv, twin, sums,
                 xrelay, xfinal, ynear, yown, brelay, bfinal, nrelay, nfinal, grads,
                 lsem, zsend, zrecv, send, recv):
    seq, mp, y, x, core = place()
    slots, zright, zleft, zfar = z_places(seq, mp)
    me, l, r, o = slots
    zsems, sems = (zsend, zrecv), (send, recv)
    xr, xl, xo = plus(x, 1), plus(x, -1), plus(x, 2)
    up, down = (seq_of(plus(y, 1), x, core), mp), (seq_of(plus(y, -1), x, core), mp)
    right, left = (seq_of(y, xr, core), mp), (seq_of(y, xl, core), mp)
    partner = (seq_of(y, x, 1 - core), mp)
    above = (seq_of(plus(y, 2), x, core), mp)
    yu, yd, yo = plus(y, 1), plus(y, -1), plus(y, 2)
    rows = [plus(y, -k) for k in range(3)]
    heads = [pl.ds(h * TOK, TOK) for h in range(4)]
    whole = pl.ds(0, TOK)

    met = greet([up, down, above, right, left, partner, zright, zleft, zfar])

    x_load = pltpu.make_async_copy(x_ref, x_buf.at[me], lsem.at[0])
    x_load.start()
    loads = []
    for n, slot in enumerate((me, l, r, o)):
        at = pl.ds(pl.multiple_of(slot * COLS, COLS), COLS)
        group = []
        for i, (w, lo, hi) in enumerate(((wq_ref, 0, 512), (wk_ref, 512, 640), (wv_ref, 640, 768))):
            copy = pltpu.make_async_copy(w.at[at], weights.at[at, pl.ds(lo, hi - lo)], lsem.at[1 + 3 * n + i])
            copy.start()
            group.append(copy)
        loads.append(group)
    g_load = pltpu.make_async_copy(g_ref, g_buf.at[me], lsem.at[13])
    g_load.start()
    w_loads = []
    for n, slot in enumerate((me, l, r, o)):
        cols = pl.ds(pl.multiple_of(slot * COLS, COLS), COLS)
        copy = pltpu.make_async_copy(wo_ref.at[:, cols], w_out.at[slot], lsem.at[14 + n])
        copy.start()
        w_loads.append(copy)
    late = []
    for i, (src, dst) in enumerate(((x_ref, x_own), (y_ref, y_own), (g2_ref, g2_own))):
        copy = pltpu.make_async_copy(src, dst, lsem.at[18 + i])
        copy.start()
        late.append(copy)

    x_rings = [
        RingGather(x_ref, x_buf, slots, i * HALF, HALF // 2, HALF, zsems, 30 * i, zright, zleft) for i in range(2)
    ]
    met()
    x_rings[0].start_first()
    x_load.wait()
    values = x_buf[me].astype(F32)
    squares = jnp.sum(values * values, axis=-1, keepdims=True)
    mine[0] = jnp.broadcast_to(squares, (TOK, 128)).T[0:8, :]

    def exchange(which, base):
        return [
            remote(mine.at[which], theirs.at[which, i], zsems, base + i, device)
            for i, device in enumerate((zright, zleft, zfar))
        ]

    small = exchange(0, 6)
    for copy in small:
        copy.start()
    x_rings[0].start_second()
    docs = docs_ref[...].astype(F32)
    kvb[seq, pl.ds(TOK, 16), :] = jnp.broadcast_to(docs, (16, TOK)).astype(BF16)

    def clear(i, carry):
        for k in range(3):
            for c in range(2):
                dkv[k, i, c] = jnp.zeros((TOK, 256), BF16)
        return carry

    lax.fori_loop(0, 4, clear, 0)
    for copy in small:
        copy.wait_recv()
    squares = mine[0] + theirs[0, 0] + theirs[0, 1] + theirs[0, 2]
    inverse = lax.rsqrt(squares[0:1, :] * (1.0 / WIDTH) + EPSILON)
    inv_ref[...] = jnp.broadcast_to(inverse, (128, TOK)).T

    def column(n, slot, i, part):
        at = pl.ds(pl.multiple_of(slot * COLS, COLS), COLS)
        cols = pl.ds(i * 256, 256)
        term = jnp.dot(scaled[part, :], weights[at, cols], preferred_element_type=F32)
        acc[part, cols] = term if n == 0 else acc[part, cols] + term

    def scale_rows(slot, part):
        gain = gain_ref[:, pl.ds(pl.multiple_of(slot * COLS, COLS), COLS)]
        scaled[part, :] = (x_buf[slot, part, :].astype(F32) * inv_ref[part, 0:1] * gain).astype(BF16)

    def fold(n, slot, part):
        scale_rows(slot, part)
        for i in range(3):
            column(n, slot, i, part)

    def fold_grad(n, slot):
        w_loads[n].wait()
        term = lax.dot_general(g_buf[slot], w_out[slot], NT, preferred_element_type=F32)
        go_acc[...] = term if n == 0 else go_acc[...] + term

    halves = (pl.ds(0, HALF), pl.ds(HALF, HALF))
    sent = (pl.ds(0, HALF), pl.ds(HALF, ROWS_KV - HALF))
    rings, across, across_in = [], [], []
    for k in range(3):
        at = [seq_of(rows[k], column_, core) for column_ in (x, xl, xr, xo)]
        there = [seq_of(rows[k], column_, 1 - core) for column_ in (x, xl, xr, xo)]
        rings.append([
            RingGather(
                kvb.at[at[0]], kvb, at, i * HALF, 64, (HALF, ROWS_KV - HALF)[i], sems, 12 * k + 6 * i, right, left
            )
            for i in range(2)
        ])
        across.append([
            [remote(kvb.at[at[n], sent[i]], kvb.at[at[n], sent[i]], sems, 36 + 8 * k + 2 * n + i, partner)
             for n in range(4)] for i in range(2)
        ])
        across_in.append([
            [remote(kvb.at[at[n], sent[i]], kvb.at[there[n], sent[i]], sems, 36 + 8 * k + 2 * n + i, partner)
             for n in range(4)] for i in range(2)
        ])
    b1, b2 = seq_of(rows[1], x, core), seq_of(rows[2], x, core)

    def lift(dst, base, device):
        return [remote(kvb.at[seq, sent[i]], kvb.at[dst, sent[i]], sems, base + i, device) for i in range(2)]

    up_own, in_own = lift(seq, 60, up), lift(b1, 60, up)
    up_next, in_next = lift(seq, 62, above), lift(b2, 62, above)

    def launch(i):
        kvb[seq, halves[i], :] = acc[halves[i], pl.ds(512, 256)].astype(BF16)
        up_own[i].start()
        up_next[i].start()
        rings[0][i].start()
        across[0][i][0].start()

    def second_row(i):
        in_own[i].wait_recv()
        rings[1][i].start()
        across[1][i][0].start()

    def third_row(i):
        in_next[i].wait_recv()
        rings[2][i].start()
        across[2][i][0].start()

    def near(k, i):
        rings[k][i].wait_left()
        across[k][i][1].start()
        rings[k][i].wait_right()
        across[k][i][2].start()

    def pass_on(k, i):
        near(k, i)
        rings[k][i].wait_far()
        across[k][i][3].start()

    g_ring = RingGather(g_ref, g_buf, slots, 0, HALF, TOK, zsems, 9, zright, zleft)
    for group in loads:
        for copy in group:
            copy.wait()
    slot = 2 * x + core
    pieces = []
    for i, (target, device) in enumerate(((r, zright), (l, zleft), (o, zfar))):
        at = pl.ds(pl.multiple_of(target * COLS + seq * 32, 32), 32)
        pieces.append(remote(weights.at[at, pl.ds(512, 256)], wkv.at[i, y, slot], zsems, 36 + i, device))
    y_pieces = RingGather(
        None, None, (y, yd, yu, yo), 0, 16, 32, sems, 87, up, down,
        at=lambda row, part: wkv.at[:, row, slot, part],
    )
    x_pieces = RingGather(
        None, None, (x, xl, xr, xo), 0, 16, 32, sems, 93, right, left,
        at=lambda column_, part: wkv.at[:, :, 2 * column_ + core, part],
    )
    over_pieces = [
        remote(wkv.at[:, :, 2 * n + core], wkv.at[:, :, 2 * n + core], sems, 99 + n, partner) for n in range(4)
    ]
    over_in = [
        remote(wkv.at[:, :, 2 * n + core], wkv.at[:, :, 2 * n + 1 - core], sems, 99 + n, partner) for n in range(4)
    ]
    x_rings[0].forward()
    for copy in pieces:
        copy.start()
    x_rings[1].start()
    fold(0, me, whole)
    x_rings[0].wait_left()
    fold(1, l, halves[0])
    x_rings[0].wait_right()
    fold(2, r, halves[0])
    x_rings[0].wait_far()
    scale_rows(o, halves[0])
    column(3, o, 2, halves[0])
    launch(0)
    x_rings[1].forward()
    g_ring.start()
    column(3, o, 0, halves[0])
    column(3, o, 1, halves[0])
    rings[0][0].forward()
    second_row(0)
    third_row(0)
    x_rings[1].wait_left()
    fold(1, l, halves[1])
    x_rings[1].wait_right()
    fold(2, r, halves[1])
    pass_on(0, 0)
    rings[1][0].forward()
    x_rings[1].wait_far()
    scale_rows(o, halves[1])
    column(3, o, 2, halves[1])
    launch(1)
    for copy in pieces:
        copy.wait_recv()
    y_pieces.start()
    rings[2][0].forward()
    column(3, o, 0, halves[1])
    column(3, o, 1, halves[1])
    pass_on(1, 0)
    for h in range(4):
        piece = acc[:, pl.ds(h * HEAD, HEAD)].astype(BF16)
        qs[heads[h], :] = piece
        qt[pl.ds(0, HEAD), heads[h]] = piece.astype(F32).T.astype(BF16)
    number = lax.broadcasted_iota(jnp.int32, (HEAD, TOK), 0).astype(F32)
    other = jnp.where(number == docs, 0.0, MASKED).astype(BF16)
    for h in range(4):
        qt[pl.ds(HEAD, HEAD), heads[h]] = other
    m_buf[...] = jnp.full(m_buf.shape, MASKED, F32)
    m_run[...] = jnp.full(m_run.shape, MASKED, F32)
    l_buf[...] = jnp.zeros(l_buf.shape, F32)
    o_acc[...] = jnp.zeros(o_acc.shape, F32)
    dq_acc[...] = jnp.zeros(dq_acc.shape, F32)

    def score(b, diagonal):
        key_docs = kvb[b, pl.ds(TOK, 16), :].astype(F32)[0:1, :]
        same = jnp.where(number == key_docs, 1.0, 0.0)
        ka[:, pl.ds(0, HEAD)] = kvb[b, whole, pl.ds(0, HEAD)]
        ka[:, pl.ds(HEAD, HEAD)] = same.T.astype(BF16)
        for h in range(4):
            s = jnp.dot(ka[...], qt[:, heads[h]], preferred_element_type=F32)
            if diagonal:
                key_at = lax.broadcasted_iota(jnp.int32, (TOK, TOK), 0)
                query_at = lax.broadcasted_iota(jnp.int32, (TOK, TOK), 1)
                s = jnp.where(key_at <= query_at, s, MASKED)
            s_buf[seq - b, :, heads[h]] = s
            m_buf[:, heads[h]] = jnp.maximum(m_buf[:, heads[h]], s.reshape(TOK // 8, 8, TOK).max(axis=0))

    def raise_top():
        top = jnp.maximum(jnp.max(m_buf[...], axis=0, keepdims=True), m_run[0:1, :])
        factor = jnp.exp2((m_run[0:1, :] - top) * (SCALE * LOG2E))
        m_run[...] = jnp.broadcast_to(top, m_run.shape)
        t_buf[...] = m_run[...] * (SCALE * LOG2E)
        l_buf[...] = l_buf[...] * factor
        o_acc[...] = o_acc[...] * factor

    def mix(b):
        values = kvb[b, whole, pl.ds(HEAD, HEAD)]
        for h in range(4):
            s = s_buf[seq - b, :, heads[h]]
            p = jnp.exp2(s * (SCALE * LOG2E) - t_buf[0:1, heads[h]])
            l_buf[:, heads[h]] += p.reshape(TOK // 8, 8, TOK).sum(axis=0)
            o_acc[:, heads[h]] += lax.dot_general(
                values, p.astype(BF16), TN, preferred_element_type=F32
            )

    def sweep(step, lo, hi):
        def one(b, carry):
            step(b)
            return carry

        lax.fori_loop(lo, hi, one, 0)

    def fold_grad_own():
        g_load.wait()
        fold_grad(0, me)

    low1 = jnp.maximum(8 * y - 8, 0)
    mid1 = jnp.maximum(8 * y - 4, 0)
    mid0 = jnp.minimum(8 * y + 4, seq)
    low2 = jnp.maximum(seq - (BAND - 1), 0)
    rings[0][1].forward()
    second_row(1)
    third_row(1)
    score(seq, True)
    pass_on(2, 0)
    pass_on(0, 1)
    y_pieces.forward()
    rings[1][1].forward()
    rings[2][1].forward()
    for copies in across_in[0]:
        for copy in copies:
            copy.wait_recv()
    sweep(lambda b: score(b, False), 8 * y, mid0)
    g_ring.forward()
    sweep(lambda b: score(b, False), mid0, seq)
    raise_top()
    pass_on(1, 1)
    sweep(mix, 8 * y, mid0)
    pass_on(2, 1)
    sweep(mix, mid0, seq + 1)
    y_pieces.wait_left()
    y_pieces.wait_right()
    y_pieces.wait_far()
    x_pieces.start()
    fold_grad_own()
    for copies in across_in[1]:
        for copy in copies:
            copy.wait_recv()
    sweep(lambda b: score(b, False), low1, 8 * y)
    raise_top()
    sweep(mix, low1, 8 * y)
    g_ring.wait_left()
    fold_grad(1, l)
    g_ring.wait_right()
    fold_grad(2, r)
    for copies in across_in[2]:
        for copy in copies:
            copy.wait_recv()
    sweep(lambda b: score(b, False), low2, low1)
    raise_top()
    sweep(mix, low2, low1)
    x_pieces.forward()
    g_ring.wait_far()
    fold_grad(3, o)
    for h in range(4):
        grad = go_acc[:, pl.ds(h * HEAD, HEAD)].astype(BF16)
        dot_buf[:, heads[h]] = grad.astype(F32).T.astype(BF16)
    g_ring.finish()

    total = jnp.sum(l_buf[...], axis=0, keepdims=True)
    inverse = 1.0 / total
    t_buf[...] = t_buf[...] + jnp.log2(total)
    for h in range(4):
        mixed = (o_acc[:, heads[h]] * inverse[:, h * TOK : (h + 1) * TOK]).astype(BF16).astype(F32)
        att[:, pl.ds(h * HEAD, HEAD)] = mixed.T.astype(BF16)
        delta = jnp.sum(dot_buf[:, heads[h]].astype(F32) * mixed, axis=0, keepdims=True)
        d_buf[:, heads[h]] = jnp.broadcast_to(delta, (8, TOK))

    def branch_term(slot):
        g_buf[slot] = jnp.dot(att[...], w_out[slot], preferred_element_type=F32).astype(BF16)

    b_ring = RingReduce(
        lambda slot, part: g_buf.at[slot, part], brelay, bfinal, slots, HALF, TOK, zsems, 15, zright, zleft
    )
    branch_term(o)
    b_ring.start_far()

    def back(b, k):
        keys = kvb[b, whole, pl.ds(0, HEAD)]
        values = kvb[b, whole, pl.ds(HEAD, HEAD)]
        for h in range(4):
            s = s_buf[seq - b, :, heads[h]]
            p = jnp.exp2(s * (SCALE * LOG2E) - t_buf[0:1, heads[h]])
            dp = jnp.dot(values, dot_buf[:, heads[h]], preferred_element_type=F32)
            p_buf[:, heads[h]] = p.astype(BF16)
            ds_buf[:, heads[h]] = (p * (dp - d_buf[0:1, heads[h]])).astype(BF16)
        dq_acc[...] += lax.dot_general(keys, ds_buf[...], TN, preferred_element_type=F32)
        value_grad = lax.dot_general(dot_buf[...], p_buf[...], NT, preferred_element_type=F32)
        key_grad = lax.dot_general(qt[pl.ds(0, HEAD), :], ds_buf[...], NT, preferred_element_type=F32)
        i = b - 8 * (y - k)
        to = dkv.at[k, lax.div(i, 2), lax.rem(i, 2)]
        to[pl.ds(0, HEAD), :] = (key_grad * SCALE).astype(BF16)
        to[pl.ds(HEAD, HEAD), :] = value_grad.astype(BF16)

    over = [remote(dkv.at[k, :, 1 - core], twin.at[k], sems, 64 + k, partner) for k in range(3)]
    sum_rings = [
        RingReduce(
            lambda slot, part, k=k: sums.at[k, slot, part],
            xrelay.at[k], xfinal.at[k], (x, xl, xr, xo), HALF, TOK, sems, 67 + 6 * k, right, left,
        )
        for k in range(3)
    ]

    def open_ring(k):
        over[k].wait_recv()

        def add(i, carry):
            sums[k, i] = (dkv[k, i, core].astype(F32) + twin[k, i].astype(F32)).astype(BF16)
            return carry

        lax.fori_loop(0, 4, add, 0)
        sum_rings[k].start_far()
        sum_rings[k].start_near()

    far_up = remote(yown.at[0], ynear.at[0], sems, 85, down)
    near_up = remote(yown.at[1], ynear.at[1], sems, 86, down)
    sweep(lambda b: back(b, 2), low2, low1)
    over[2].start()
    branch_term(r)
    branch_term(l)
    b_ring.start_near()
    sweep(lambda b: back(b, 1), low1, mid1)
    open_ring(2)
    b_ring.forward()
    sweep(lambda b: back(b, 1), mid1, 8 * y)
    over[1].start()
    sweep(lambda b: back(b, 0), 8 * y, mid0)
    sum_rings[2].forward()
    sweep(lambda b: back(b, 0), mid0, seq + 1)
    over[0].start()
    grads_q = dq_acc[...] * SCALE
    for h in range(4):
        grads[:, pl.ds(h * HEAD, HEAD)] = grads_q[:, h * TOK : (h + 1) * TOK].T.astype(BF16)
    for ring in x_rings:
        ring.finish()

    def norm_term(slot):
        for i in range(4):
            at = pl.ds(pl.multiple_of(slot * COLS + i * 256, 256), 256)
            piece = lax.dot_general(
                grads[:, pl.ds(0, 512)], weights[at, pl.ds(0, 512)], NT, preferred_element_type=F32
            )
            x_buf[slot, :, pl.ds(i * 256, 256)] = piece.astype(BF16)

    n_ring = RingReduce(
        lambda slot, part: x_buf.at[slot, part], nrelay, nfinal, slots, HALF, TOK, zsems, 21, zright, zleft
    )
    norm_term(o)
    n_ring.start_far()
    open_ring(1)
    norm_term(r)
    norm_term(l)
    n_ring.start_near()
    yown[0] = sum_rings[2].wait_total()(whole).astype(BF16)
    far_up.start()
    open_ring(0)
    sum_rings[1].forward()
    x_pieces.wait_left()
    x_pieces.wait_right()
    x_pieces.wait_far()
    for copy in over_pieces:
        copy.start()
    total = sum_rings[1].wait_total()(whole)
    far_up.wait_recv()
    yown[1] = (total + ynear[0].astype(F32)).astype(BF16)
    near_up.start()
    sum_rings[0].forward()
    branch_term(me)
    norm_term(me)
    dots = jnp.zeros((TOK, 1), F32)
    for h in range(4):
        dots += jnp.sum(
            qs[heads[h], :].astype(F32) * grads[:, pl.ds(h * HEAD, HEAD)].astype(F32), axis=-1, keepdims=True
        )
    for copy in late:
        copy.wait()
    total = b_ring.wait_total()
    for part in (pl.ds(0, HALF), pl.ds(HALF, HALF)):
        s_buf[0, part, :] = y_own[part, :].astype(F32) - total(part)
    first_out = pltpu.make_async_copy(s_buf.at[0], first_ref, lsem.at[21])
    first_out.start()
    n_ring.forward()
    total = sum_rings[0].wait_total()(whole)
    near_up.wait_recv()
    total = (total + ynear[1].astype(F32)).astype(BF16).astype(F32).T
    kv_all[me] = total.astype(BF16)
    kv_ring = RingGather(None, kv_all, slots, 0, HALF, TOK, zsems, 39, zright, zleft)
    kv_ring.start()
    dots += jnp.sum(kvb[seq, whole, :].astype(F32) * kv_all[me].astype(F32), axis=-1, keepdims=True)
    mine[1] = jnp.broadcast_to(dots, (TOK, 128)).T[0:8, :]
    small_dots = exchange(1, 27)
    for copy in small_dots:
        copy.start()

    for copy in over_in:
        copy.wait_recv()

    def kv_term(n, slot):
        for i in range(4):
            cols = pl.ds(i * 256, 256)
            if n == 0:
                at = pl.ds(pl.multiple_of(me * COLS + i * 256, 256), 256)
                w = weights[at, pl.ds(512, 256)]
            else:
                w = wkv[n - 1, i].reshape(256, 256)
            term = lax.dot_general(kv_all[slot], w, NT, preferred_element_type=F32)
            s_buf[2, :, cols] = term if n == 0 else s_buf[2, :, cols] + term

    kv_term(0, me)
    kv_ring.forward()
    kv_ring.wait_left()
    kv_term(1, l)
    kv_ring.wait_right()
    kv_term(2, r)
    for copy in small_dots:
        copy.wait_recv()
    mean = (mine[1] + theirs[1, 0] + theirs[1, 1] + theirs[1, 2])[0:1, :] * (1.0 / WIDTH)
    mean = jnp.broadcast_to(mean, (128, TOK)).T
    gain = gain_ref[:, pl.ds(pl.multiple_of(me * COLS, COLS), COLS)]
    total = n_ring.wait_total()
    kv_ring.wait_far()
    kv_term(3, o)
    grad_out = []
    for i in range(2):
        lo, hi, part = i * HALF, (i + 1) * HALF, pl.ds(i * HALF, HALF)
        inverse = inv_ref[part, 0:1]
        unit = x_own[part, :].astype(F32) * inverse
        s_buf[1, part, :] = g2_own[part, :].astype(F32) + inverse * (
            (total(part) + s_buf[2, part, :]) * gain - unit * mean[lo:hi, 0:1]
        )
        copy = pltpu.make_async_copy(s_buf.at[1, part], grad_ref.at[part], lsem.at[22 + i])
        copy.start()
        grad_out.append(copy)
    first_out.wait()
    for copy in grad_out:
        copy.wait()
    for copy in small + small_dots + pieces + over_pieces + over + [far_up, near_up] + up_own + up_next:
        copy.wait_send()
    for ring in rings[0] + rings[1] + rings[2] + sum_rings + [b_ring, n_ring, kv_ring, y_pieces, x_pieces]:
        ring.finish()
    for k in range(3):
        for i in range(2):
            for copy in across[k][i]:
                copy.wait_send()


def block(x, g, y, g2, docs, gain, w_query, w_key, w_value, w_out):
    return pl.pallas_call(
        block_kernel,
        name="block",
        out_shape=(
            jax.ShapeDtypeStruct((TOK, COLS), F32),
            jax.ShapeDtypeStruct((TOK, COLS), F32),
        ),
        in_specs=[ANY, ANY, ANY, ANY, VM, VM, ANY, ANY, ANY, ANY],
        out_specs=(ANY, ANY),
        scratch_shapes=[
            pltpu.VMEM((TOK, 128), F32),
            pltpu.VMEM((TOK, COLS), BF16),
            pltpu.VMEM((TOK, COLS), BF16),
            pltpu.VMEM((TOK, COLS), BF16),
            pltpu.VMEM((TOK, 1024), BF16),
            pltpu.VMEM((TOK, 1024), BF16),
            pltpu.VMEM((3, 4, 8, 32, 256), BF16),
            pltpu.VMEM((4, TOK, 256), BF16),
            pltpu.VMEM((4, TOK, COLS), BF16),
            pltpu.VMEM((4, TOK, COLS), BF16),
            pltpu.VMEM((WIDTH, 768), BF16),
            pltpu.VMEM((4, 512, COLS), BF16),
            pltpu.VMEM((TOK, 768), F32),
            pltpu.VMEM((TOK, 512), F32),
            pltpu.VMEM((TOK, COLS), BF16),
            pltpu.VMEM((2, 8, TOK), F32),
            pltpu.VMEM((2, 3, 8, TOK), F32),
            pltpu.VMEM((32, ROWS_KV, 256), BF16),
            pltpu.VMEM((BAND, TOK, 1024), F32),
            pltpu.VMEM((TOK, 256), BF16),
            pltpu.VMEM((256, 1024), BF16),
            pltpu.VMEM((1024, HEAD), BF16),
            pltpu.VMEM((HEAD, 1024), BF16),
            pltpu.VMEM((HEAD, 1024), F32),
            pltpu.VMEM((HEAD, 1024), F32),
            pltpu.VMEM((8, 1024), F32),
            pltpu.VMEM((8, 1024), F32),
            pltpu.VMEM((8, 1024), F32),
            pltpu.VMEM((8, 1024), F32),
            pltpu.VMEM((8, 1024), F32),
            pltpu.VMEM((TOK, 512), BF16),
            pltpu.VMEM((3, 4, 2, TOK, 256), BF16),
            pltpu.VMEM((3, 4, TOK, 256), BF16),
            pltpu.VMEM((3, 4, TOK, 256), BF16),
            pltpu.VMEM((3, 2, HALF, 256), BF16),
            pltpu.VMEM((3, 2, TOK, 256), BF16),
            pltpu.VMEM((2, TOK, 256), BF16),
            pltpu.VMEM((2, TOK, 256), BF16),
            pltpu.VMEM((2, HALF, COLS), BF16),
            pltpu.VMEM((2, TOK, COLS), BF16),
            pltpu.VMEM((2, HALF, COLS), BF16),
            pltpu.VMEM((2, TOK, COLS), BF16),
            pltpu.VMEM((TOK, 512), BF16),
            DMA((24,)),
            DMA((45,)),
            DMA((45,)),
            DMA((103,)),
            DMA((103,)),
        ],
        compiler_params=pltpu.CompilerParams(
            collective_id=0, has_side_effects=True, vmem_limit_bytes=63 * MIB
        ),
    )(x, g, y, g2, docs, gain, w_query, w_key, w_value, w_out)


def hand_on_kernel(a_ref, b_ref, a_out, b_out, a_buf, b_buf, sem):
    moves = []
    for n, (src, buf, dst) in enumerate(((a_ref, a_buf, a_out), (b_ref, b_buf, b_out))):
        for i in range(2):
            part = pl.ds(i * HALF, HALF)
            take = pltpu.make_async_copy(src.at[part], buf.at[part], sem.at[0, n, i])
            give = pltpu.make_async_copy(buf.at[part], dst.at[part], sem.at[1, n, i])
            take.start()
            moves.append((take, give))
    for take, give in moves:
        take.wait()
        give.start()
    for take, give in moves:
        give.wait()


def hand_on(a, b):
    shape = jax.ShapeDtypeStruct((TOK, COLS), F32)
    return pl.pallas_call(
        hand_on_kernel,
        name="hand_on",
        out_shape=(shape, shape),
        in_specs=[ANY, ANY],
        out_specs=(ANY, ANY),
        scratch_shapes=[
            pltpu.VMEM((TOK, COLS), F32),
            pltpu.VMEM((TOK, COLS), F32),
            DMA((2, 2, 2)),
        ],
        compiler_params=pltpu.CompilerParams(vmem_limit_bytes=63 * MIB),
    )(a, b)


def per_device(
    y_first, x_second, grad_first, grad_second, doc_ids, norm_gain, w_query, w_key, w_value, w_out
):
    first, grad = block(
        x_second, grad_first, y_first, grad_second, doc_ids.reshape(1, TOK), norm_gain.reshape(1, WIDTH),
        w_query, w_key, w_value, w_out,
    )
    return hand_on(first, grad)


def solution(mesh):
    placed = (
        P("seq", "mp"),
        P("seq", "mp"),
        P("seq", "mp"),
        P("seq", "mp"),
        P("seq"),
        P(),
        P(None, "mp"),
        P(None, "mp"),
        P(None, "mp"),
        P("mp", None),
    )
    return jax.shard_map(
        per_device,
        mesh=mesh,
        in_specs=placed,
        out_specs=(P("seq", "mp"), P("seq", "mp")),
        check_vma=False,
    )
```
